32 devices in a mesh: rep: 2 (over y), ep: 16 (over z, x, core).
Axes of the slice: x: 2, y: 2, z: 4, core: 2. Of those that a mesh axis runs over, the one named last changes fastest.
Arguments:
- gen_cache: bfloat16 [256, 32, 2, 4, 128], P(('rep', 'ep')), may hold values from -6 to 6
- prompt_cache: bfloat16 [256, 2, 4, 128], replicated, may hold values from -5 to 5
- ancestors: int32 [256], P(('rep', 'ep')), may hold values from 0 to 127, as said below
- queries: bfloat16 [256, 2, 64, 128], P(('rep', 'ep')), may hold values from -5 to 5
- new_kv: bfloat16 [256, 2, 2, 4, 128], P(('rep', 'ep')), may hold values from -6 to 6
- tokens_in: bfloat16 [256, 2, 2048], P(('rep', 'ep')), may hold values from -6 to 6
- norm_gain: float32 [2048], replicated, may hold values from 0.1 to 1.9
- routes: int32 [2, 128, 2, 8], P(None, 'ep'), may hold values from 0 to 15, all different within a row; in each aligned block of 16 rows (0 to 15, 16 to 31, ..., all dimensions but the last counted through in order) at most 16 rows name the same one
- gate_weights: float32 [2, 128, 2, 8], P(None, 'ep'), may hold values from 0.1 to 1
- w_gate_up: bfloat16 [16, 2048, 2, 768], P('ep', None, None, 'rep'), may hold values from -0.125 to 0.125
- w_down: bfloat16 [16, 768, 2048], P('ep', 'rep'), may hold values from -0.21875 to 0.21875
Outputs:
- cache_out: bfloat16 [256, 32, 2, 4, 128], P(('rep', 'ep'))
- attn_out: bfloat16 [256, 2, 64, 128], P(('rep', 'ep'))
- expert_out: bfloat16 [256, 2, 2048], P(('rep', 'ep'))
The draws below stay inside these ranges and needn't reach their ends.
Inputs may be any that keep to these rules, and one draw needn't show every extreme that they name: The parent of particle p is particle (p // 128) * 128 + ancestors[p]. `routes`: each row names 8 different experts. In the rows of one device (aligned blocks of 16 rows, taking the leading dimensions together in order) no expert is named more than 16 times.
All inputs are finite; a program needn't handle non-finite values.
Results may differ from the reference program's by a relative error of at most 0.013.
Values may be sent and summed in bfloat16 or wider, within the bound.
A program may use at most 64 MiB of HBM per device.

```python
import functools
import math
import jax
import jax.numpy as jnp
import numpy as np
from jax import lax

D = 2048
HID = 768
QH = 64
KVH = 4
HD = 128
TOP = 8
P_SIZE = 256
G = 32
PD = 8
GROUP = 128
PARTICLES = 256
EXPERTS = 16
HSLICE = 384
MOST = 16
N_REP = 2
DEVICES = 32


def query_parts(key):
    base = jnp.clip(jax.random.normal(jax.random.fold_in(key, 101), (PARTICLES, 2, QH, HD), jnp.float32), -5.0, 5.0)
    final = base
    return (base, final)


def draw_queries(key, part):
    return query_parts(key)[1].astype(jnp.bfloat16)


def draw_new_kv(key, part):
    base = query_parts(key)[0]
    grouped = jnp.mean(base.reshape(PARTICLES, 2, KVH, QH // KVH, HD), axis=3)
    noise = jax.random.normal(jax.random.fold_in(key, 111), (PARTICLES, 2, KVH, HD), jnp.float32)
    new_keys = jnp.clip(4.0 * grouped + 0.5 * noise, -6.0, 6.0)
    new_values = jnp.clip(jax.random.normal(jax.random.fold_in(key, 112), (PARTICLES, 2, KVH, HD), jnp.float32), -6.0, 6.0)
    return jnp.stack([new_keys, new_values], axis=2).astype(jnp.bfloat16)


def draw_prompt_cache(key, part):
    values = jnp.clip(jax.random.normal(jax.random.fold_in(key, 121), (P_SIZE, 2, KVH, HD), jnp.float32), -5.0, 5.0)
    return values.astype(jnp.bfloat16)


def draw_ancestors(key, part):
    groups = PARTICLES // GROUP
    first = jax.random.randint(jax.random.fold_in(key, 201), (PARTICLES,), 0, GROUP, dtype=jnp.int32)
    second = jax.random.randint(jax.random.fold_in(key, 202), (PARTICLES,), 0, GROUP, dtype=jnp.int32)
    skewed = first * second // GROUP
    even = jax.random.randint(jax.random.fold_in(key, 203), (PARTICLES,), 0, GROUP, dtype=jnp.int32)
    coins = jax.random.randint(jax.random.fold_in(key, 204), (PARTICLES,), 0, 2, dtype=jnp.int32)
    picked = jnp.where(coins == 1, skewed, even)
    labels = jax.vmap(lambda subkey: jax.random.permutation(subkey, GROUP))(jax.random.split(jax.random.fold_in(key, 205), groups)).astype(jnp.int32)
    group_of = jnp.arange(PARTICLES, dtype=jnp.int32) // GROUP
    local = jnp.arange(PARTICLES, dtype=jnp.int32) % GROUP
    result = labels[group_of, picked]
    spot_high = jax.random.randint(jax.random.fold_in(key, 206), (groups,), 0, GROUP, dtype=jnp.int32)
    offset = jax.random.randint(jax.random.fold_in(key, 207), (groups,), 1, GROUP, dtype=jnp.int32)
    spot_low = (spot_high + offset) % GROUP
    result = jnp.where(local == spot_high[group_of], GROUP - 1, result)
    result = jnp.where(local == spot_low[group_of], 0, result)
    return result.astype(jnp.int32)


def levels(own_key, dims, cuts, smallest, largest):
    loudness, own = 1.0, jax.random.fold_in(own_key, 6)
    for axis_at, blocks in cuts:
        heights = jnp.exp(jax.random.uniform(jax.random.fold_in(own, axis_at), (blocks,), jnp.float32, smallest / len(cuts), largest / len(cuts)))
        loudness = loudness * jnp.repeat(heights, dims[axis_at] // blocks).reshape([-1 if axis == axis_at else 1 for axis in range(len(dims))])
    return loudness


def shared_out(rng, own, number, rows, number_of, top, reach, slope):
    ranking = jax.random.permutation(rng, number_of)
    packed, ordinary = shares(number_of, rows * top, reach, slope, True), shares(number_of, rows * top, reach, slope, False)
    places = jnp.arange(number_of)

    def named(sizes, turn):
        used = int((sizes > 0).sum())
        fixed = max(1, used // 4)
        shifted = fixed + (places - fixed + turn * (used - fixed)) % max(1, number_of - fixed)
        return jnp.zeros((number_of,), jnp.int32).at[ranking[jnp.where(places < fixed, places, shifted)]].set(jnp.asarray(sizes, jnp.int32))

    sizes = jnp.where(number % 4 == 0, named(packed, number // 4), named(ordinary, number - number // 4 - 1))
    mixed = jax.random.permutation(jax.random.fold_in(own, 3), number_of)
    source_of, receiver = mixed[0:number_of // 2 * 2:2], mixed[1:number_of // 2 * 2:2]
    slack = jnp.minimum(sizes[source_of] - 1, reach - sizes[receiver]) // 2
    slack = jnp.where((source_of == ranking[0]) | (receiver == ranking[0]) | (sizes[receiver] == 0), 0, jnp.maximum(slack, 0))
    shifted = jax.random.randint(jax.random.fold_in(own, 4), (number_of // 2,), 0, 1 << 20) % (slack + 1)
    sizes = sizes.at[source_of].add(-shifted).at[receiver].add(shifted)
    items = jnp.searchsorted(jnp.cumsum(sizes), jnp.arange(rows * top), side="right").astype(jnp.int32)
    table = items.reshape(top, rows).T
    table = table[jax.random.permutation(jax.random.fold_in(own, 1), rows)]
    turn = jax.random.randint(jax.random.fold_in(own, 2), (rows, 1), 0, top)
    return jnp.take_along_axis(table, (jnp.arange(top)[None, :] + turn) % top, axis=1)


def shares(count, total, most, skew, full):
    weights = [(1 << 20) // math.isqrt(standing ** skew) + 1 for standing in range(1, count + 1)]
    largest = most if full else min(most, max(-(-total // count), total * weights[0] // sum(weights)))
    least = 1 if total - largest >= count - 1 else 0
    given, spare = [largest] + [least] * (count - 1), total - largest - least * (count - 1)
    while spare > 0:
        movable = [i for i in range(1, count) if given[i] < largest] or [i for i in range(1, count) if given[i] < most]
        pool, left = sum([weights[i] for i in movable]), spare
        for i in movable:
            addition = min(most - given[i], max(1, left * weights[i] // pool), spare)
            given[i] = given[i] + addition
            spare = spare - addition
    return np.array(given)


def scatter_about(key, dims, spread, reach, cuts=(), held_as=jnp.bfloat16):
    gain = levels(key, dims, cuts, -0.22, 0.18) if cuts else 1.0
    entries = jax.random.normal(key, dims, jnp.float32) * spread * gain
    return jnp.minimum(jnp.maximum(entries, -reach), reach).astype(held_as)


def setup_inputs(seed: int = 0) -> dict:
    keys = jax.random.split(jax.random.key(seed), 12)
    gen_cache = scatter_about(keys[0], (PARTICLES, G, 2, KVH, HD), 1.0, 6.0, ((0, 32),))
    prompt_cache = draw_prompt_cache(jax.random.fold_in(keys[11], 71), 0)
    ancestors = draw_ancestors(jax.random.fold_in(keys[11], 71), 0)
    queries = draw_queries(jax.random.fold_in(keys[11], 71), 0)
    new_kv = draw_new_kv(jax.random.fold_in(keys[11], 71), 0)
    tokens_in = scatter_about(keys[5], (PARTICLES, 2, D), 1.0, 6.0, ((0, 32),))
    norm_gain = jnp.clip(1.0 + 0.18 * jax.random.normal(keys[6], (D,), jnp.float32), 0.1, 1.9)
    routes_keys = jax.random.split(jax.random.fold_in(keys[7], 1), N_REP * GROUP * 2 // (2 * PD))
    routes_turns = jax.random.permutation(jax.random.fold_in(keys[7], 3), N_REP * GROUP * 2 // (2 * PD))
    routes = jax.vmap(lambda own, number: shared_out(jax.random.fold_in(keys[7], 2), own, number, 2 * PD, EXPERTS, TOP, MOST, 2))(routes_keys, routes_turns).reshape((N_REP, GROUP, 2, TOP))
    gate_weights = jnp.clip(jnp.exp(math.log(1.0) - 2.3025851 * jax.random.uniform(keys[8], (N_REP, GROUP, 2, TOP), jnp.float32) ** levels(keys[8], (N_REP, GROUP, 2, TOP), ((1, 16),), -0.2, 0.2)), 0.1, 1.0)
    w_gate_up = scatter_about(keys[9], (EXPERTS, D, 2, HID), D ** -0.5, 0.125, ((0, 16), (3, 2)))
    w_down = scatter_about(keys[10], (EXPERTS, HID, D), HID ** -0.5, 0.21875, ((0, 16), (1, 2)))
    return {"gen_cache": gen_cache, "prompt_cache": prompt_cache, "ancestors": ancestors, "queries": queries, "new_kv": new_kv, "tokens_in": tokens_in, "norm_gain": norm_gain, "routes": routes, "gate_weights": gate_weights, "w_gate_up": w_gate_up, "w_down": w_down}


def attend_block(inputs, prompt_cache):
    queries, gen_block, new_block = inputs
    count = queries.shape[0]
    group_heads = QH // KVH
    score_scale = 1.0 / math.sqrt(HD)
    query_f = queries.astype(jnp.float32).reshape(count, 2, KVH, group_heads, HD)
    prompt_keys = prompt_cache[:, 0].astype(jnp.float32)
    prompt_values = prompt_cache[:, 1].astype(jnp.float32)
    gen_keys = gen_block[:, :, 0].astype(jnp.float32)
    gen_values = gen_block[:, :, 1].astype(jnp.float32)
    new_keys = new_block[:, :, 0].astype(jnp.float32)
    new_values = new_block[:, :, 1].astype(jnp.float32)
    prompt_scores = jnp.einsum('btngd,snd->btngs', query_f, prompt_keys) * score_scale
    gen_scores = jnp.einsum('btngd,bsnd->btngs', query_f, gen_keys) * score_scale
    new_scores = jnp.einsum('btngd,bsnd->btngs', query_f, new_keys) * score_scale
    causal = lax.broadcasted_iota(jnp.int32, (2, 2), 1) <= lax.broadcasted_iota(jnp.int32, (2, 2), 0)
    new_scores = jnp.where(causal[None, :, None, None, :], new_scores, -jnp.inf)
    row_max = jnp.maximum(jnp.maximum(prompt_scores.max(-1), gen_scores.max(-1)), new_scores.max(-1))[..., None]
    prompt_exp = jnp.exp(prompt_scores - row_max)
    gen_exp = jnp.exp(gen_scores - row_max)
    new_exp = jnp.exp(new_scores - row_max)
    denom = (prompt_exp.sum(-1) + gen_exp.sum(-1) + new_exp.sum(-1))[..., None]
    prompt_weights = lax.optimization_barrier((prompt_exp / denom).astype(jnp.bfloat16)).astype(jnp.float32)
    gen_weights = lax.optimization_barrier((gen_exp / denom).astype(jnp.bfloat16)).astype(jnp.float32)
    new_weights = lax.optimization_barrier((new_exp / denom).astype(jnp.bfloat16)).astype(jnp.float32)
    result = jnp.einsum('btngs,snd->btngd', prompt_weights, prompt_values)
    result = result + jnp.einsum('btngs,bsnd->btngd', gen_weights, gen_values)
    result = result + jnp.einsum('btngs,bsnd->btngd', new_weights, new_values)
    return result.reshape(count, 2, QH, HD).astype(jnp.bfloat16)

def reference(gen_cache, prompt_cache, ancestors, queries, new_kv, tokens_in, norm_gain, routes, gate_weights, w_gate_up, w_down):
    particle_ids = jnp.arange(PARTICLES, dtype=jnp.int32)
    parent = (particle_ids // GROUP * GROUP + ancestors).astype(jnp.int32)
    cache_out = jnp.take(gen_cache, parent, axis=0)
    blocks = PARTICLES // PD
    inputs = (queries.reshape(blocks, PD, 2, QH, HD), cache_out.reshape(blocks, PD, G, 2, KVH, HD), new_kv.reshape(blocks, PD, 2, 2, KVH, HD))
    attn_out = lax.map(functools.partial(attend_block, prompt_cache=prompt_cache), inputs).reshape(PARTICLES, 2, QH, HD)
    row_count = PARTICLES * 2
    values_f = tokens_in.astype(jnp.float32).reshape(row_count, D)
    normed = (values_f * lax.rsqrt(lax.optimization_barrier(jnp.mean(values_f * values_f, axis=-1, keepdims=True)) + 1e-06) * norm_gain).astype(jnp.bfloat16)
    route_flat = routes.reshape(row_count * TOP).astype(jnp.int32)
    weight_flat = gate_weights.reshape(row_count * TOP)
    capacity = min(row_count, DEVICES * MOST)

    def one_expert(summed, expert):
        chosen = route_flat == expert
        found = jnp.sum(chosen.astype(jnp.int32))
        positions = jnp.nonzero(chosen, size=capacity, fill_value=0)[0].astype(jnp.int32)
        valid = jnp.arange(capacity, dtype=jnp.int32) < found
        rows = (positions // TOP).astype(jnp.int32)
        gates = jnp.where(valid, jnp.take(weight_flat, positions), 0.0)
        inputs_e = jnp.take(normed, rows, axis=0)
        weights_e = lax.dynamic_index_in_dim(w_gate_up, expert, 0, keepdims=False)
        gate = jnp.dot(inputs_e, weights_e[:, 0, :], preferred_element_type=jnp.float32)
        upward = jnp.dot(inputs_e, weights_e[:, 1, :], preferred_element_type=jnp.float32)
        act = (jax.nn.silu(gate) * upward).astype(jnp.bfloat16)
        down_e = lax.dynamic_index_in_dim(w_down, expert, 0, keepdims=False)
        parts = jnp.einsum('crh,rhd->crd', act.astype(jnp.float32).reshape(capacity, N_REP, HSLICE), down_e.astype(jnp.float32).reshape(N_REP, HSLICE, D))
        parts = parts.astype(jnp.bfloat16).astype(jnp.float32)
        full = lax.optimization_barrier(jnp.sum(parts, axis=1)) * gates[:, None]
        return (summed.at[rows].add(full), None)
    start = jnp.zeros((row_count, D), jnp.float32)
    summed, _ = lax.scan(one_expert, start, jnp.arange(EXPERTS, dtype=jnp.int32))
    expert_out = summed.astype(jnp.bfloat16).reshape(PARTICLES, 2, D)
    return (cache_out, attn_out, expert_out)
```

```python
import functools
import math

import jax
import jax.numpy as jnp
from jax import lax
from jax.experimental import pallas as pl
from jax.experimental.pallas import tpu as pltpu
from jax.sharding import PartitionSpec as P

MESH = pl.DeviceIdType.MESH
PARTS = 2
SPLIT = True
ORDER = (
    "10", "11", "12", "13", "14", "15", "16", "17",
    "W0", "F0", "W1", "O1", "O2", "O3", "G0", "W2",
    "F1", "X0", "G1", "F2", "g0", "X1", "f0", "G2",
    "F3", "g1", "X2", "z0", "f1", "G3", "g2", "P0",
    "H0", "20", "21", "22", "23", "X3", "z1", "f2",
    "g3", "H1", "24", "25", "26", "27", "z2", "f3",
    "z3", "A0", "E0",
)


def attend(queries, gen_block, new_block, prompt_cache):
    count = queries.shape[0]
    heads = queries.shape[2]
    head_dim = queries.shape[3]
    kv_heads = new_block.shape[3]
    score_scale = 1.0 / math.sqrt(head_dim)
    grouped = queries.reshape(count, 2, kv_heads, heads // kv_heads, head_dim)
    prompt_scores = (
        jnp.einsum(
            "btngd,snd->btngs", grouped, prompt_cache[:, 0], preferred_element_type=jnp.float32
        )
        * score_scale
    )
    gen_scores = (
        jnp.einsum(
            "btngd,bsnd->btngs", grouped, gen_block[:, :, 0], preferred_element_type=jnp.float32
        )
        * score_scale
    )
    new_scores = (
        jnp.einsum(
            "btngd,bsnd->btngs", grouped, new_block[:, :, 0], preferred_element_type=jnp.float32
        )
        * score_scale
    )
    causal = lax.broadcasted_iota(jnp.int32, (2, 2), 1) <= lax.broadcasted_iota(
        jnp.int32, (2, 2), 0
    )
    new_scores = jnp.where(causal[None, :, None, None, :], new_scores, -jnp.inf)
    row_max = jnp.maximum(
        jnp.maximum(prompt_scores.max(-1), gen_scores.max(-1)), new_scores.max(-1)
    )[..., None]
    prompt_exp = jnp.exp(prompt_scores - row_max)
    gen_exp = jnp.exp(gen_scores - row_max)
    new_exp = jnp.exp(new_scores - row_max)
    denom = (prompt_exp.sum(-1) + gen_exp.sum(-1) + new_exp.sum(-1))[..., None]
    prompt_weights = (prompt_exp / denom).astype(jnp.bfloat16)
    gen_weights = (gen_exp / denom).astype(jnp.bfloat16)
    new_weights = (new_exp / denom).astype(jnp.bfloat16)
    result = jnp.einsum(
        "btngs,snd->btngd", prompt_weights, prompt_cache[:, 1], preferred_element_type=jnp.float32
    )
    result = result + jnp.einsum(
        "btngs,bsnd->btngd", gen_weights, gen_block[:, :, 1], preferred_element_type=jnp.float32
    )
    result = result + jnp.einsum(
        "btngs,bsnd->btngd", new_weights, new_block[:, :, 1], preferred_element_type=jnp.float32
    )
    return result.reshape(count, 2, heads, head_dim).astype(jnp.bfloat16)


def slot_numbers(expert_ids, capacity):
    flat_ids = expert_ids.reshape(-1)
    place = jnp.arange(flat_ids.shape[0], dtype=jnp.int32)
    earlier = place[None, :] < place[:, None]
    same = flat_ids[None, :] == flat_ids[:, None]
    rank = jnp.sum((same & earlier).astype(jnp.int32), axis=1)
    return (flat_ids * capacity + rank).reshape(expert_ids.shape)


def pack_rows(rows, slot_ids, slot_count):
    selector = (
        (jnp.arange(slot_count, dtype=jnp.int32)[:, None, None] == slot_ids[None, :, :])
        .any(-1)
        .astype(jnp.bfloat16)
    )
    return jnp.dot(selector, rows, preferred_element_type=jnp.float32).astype(jnp.bfloat16)


def routed_shards(
    gen_cache,
    prompt_cache,
    ancestors,
    queries,
    new_kv,
    tokens_in,
    norm_gain,
    routes,
    gate_weights,
    w_gate_up,
    w_down,
):
    ep_count = lax.axis_size("ep")
    rep_count = lax.axis_size("rep")
    per_dev = gen_cache.shape[0]
    width = tokens_in.shape[2]
    top_count = routes.shape[3]
    parents = lax.all_gather(ancestors, "ep", axis=0, tiled=True)
    piece_len = gen_cache.size // (per_dev * ep_count)
    flat_cache = gen_cache.reshape(per_dev, ep_count, piece_len)
    chosen = jnp.take(
        lax.all_to_all(flat_cache, "ep", split_axis=1, concat_axis=0, tiled=True), parents, axis=0
    )
    moved = lax.all_to_all(chosen, "ep", split_axis=0, concat_axis=1, tiled=True)
    cache_out = moved.reshape(gen_cache.shape)
    attn_out = attend(queries, cache_out, new_kv, prompt_cache)
    values_f = tokens_in.astype(jnp.float32).reshape(per_dev * 2, width)
    normed = (
        values_f
        * lax.rsqrt(jnp.mean(values_f * values_f, axis=-1, keepdims=True) + 1e-06)
        * norm_gain
    ).astype(jnp.bfloat16)
    half_cols = w_down.shape[1]
    weight_in = w_gate_up.reshape(width, 2 * half_cols)
    weight_out = w_down.reshape(half_cols, width)
    per_expert = min(2 * per_dev, 2 * ((2 * per_dev * top_count + ep_count - 1) // ep_count))
    rep_place = lax.axis_index("rep")
    own_routes = lax.dynamic_index_in_dim(routes, rep_place, 0, keepdims=False).reshape(
        -1, top_count
    )
    own_gates = lax.dynamic_index_in_dim(gate_weights, rep_place, 0, keepdims=False).reshape(
        -1, top_count
    )
    slot_ids = slot_numbers(own_routes, per_expert)
    outgoing = pack_rows(normed, slot_ids, ep_count * per_expert).reshape(
        ep_count, per_expert, width
    )
    received = lax.all_to_all(outgoing, "ep", split_axis=0, concat_axis=0, tiled=True)
    all_rows = lax.all_gather(received, "rep", axis=0, tiled=True)
    gate_up = jnp.dot(all_rows.reshape(-1, width), weight_in, preferred_element_type=jnp.float32)
    act = (jax.nn.silu(gate_up[:, :half_cols]) * gate_up[:, half_cols:]).astype(jnp.bfloat16)
    produced = (
        jnp.dot(act, weight_out, preferred_element_type=jnp.float32)
        .astype(jnp.bfloat16)
        .reshape(all_rows.shape)
    )
    parts_back = lax.all_to_all(produced, "rep", split_axis=0, concat_axis=0, tiled=True)
    added = jnp.sum(parts_back.astype(jnp.float32).reshape((rep_count,) + received.shape), axis=0)
    came_back = (
        lax.all_to_all(added.astype(jnp.bfloat16), "ep", split_axis=0, concat_axis=0, tiled=True)
        .astype(added.dtype)
        .reshape(-1, width)
    )
    picked = jnp.take(came_back, slot_ids, axis=0)
    summed = jnp.sum(own_gates[:, :, None] * picked, axis=1)
    expert_out = summed.astype(jnp.bfloat16).reshape(per_dev, 2, width)
    return (cache_out, attn_out, expert_out)


def flip(value, mask):
    out, bit = value, 1
    while bit <= mask:
        if mask & bit:
            out = out + bit - 2 * bit * ((value // bit) % 2)
        bit *= 2
    return out


def fused_kernel(
    ep_count,
    per_dev,
    heads,
    tok_in,
    gain_ref,
    routes_ref,
    gates_ref,
    anc_ref,
    new_ref,
    cache_ref,
    q_hbm,
    prompt_hbm,
    win_hbm,
    wout_hbm,
    cache_out,
    attn_out,
    exp_out,
    tok_f,
    top_i,
    top_f,
    rows_buf,
    part,
    ra,
    rb1,
    rb2,
    rc,
    anc_buf,
    anc_smem,
    piece_buf,
    chosen,
    win_raw,
    win,
    wout,
    q_ref,
    prompt_raw,
    wide,
    prompt_ref,
    gen_ref,
    own_ref,
    w_sem,
    ag_send,
    ag_recv,
    anc_send,
    anc_recv,
    c1_send,
    c1_recv,
    c2_send,
    c2_recv,
    rs_send,
    rs_recv,
):
    r = lax.axis_index("rep")
    e = lax.axis_index("ep")
    nz = ep_count // 4
    blk = rows_buf.shape[1]
    width = gain_ref.shape[1]
    hid = wout.shape[0]
    hd = q_ref.shape[-1]
    kvh = heads[1]
    kv_rows = 2 * kvh
    c = e % 2
    swap = c if SPLIT else 0
    xstep = 2 - 4 * ((e // 2) % 2)
    ystep = 1 - 2 * r
    f_dev = (r + swap * ystep, e + (1 - swap) * xstep)
    g_dev = (r + (1 - swap) * ystep, e + swap * xstep)
    partner = (r, e + 1 - 2 * c)

    def z_dev(dz):
        return (r, flip(e // 4, dz) * 4 + e % 4)

    def remote(src, dst, ssem, rsem, dev):
        return pltpu.make_async_remote_copy(
            src_ref=src, dst_ref=dst, send_sem=ssem, recv_sem=rsem, device_id=dev, device_id_type=MESH
        )

    win_copies = [
        pltpu.make_async_copy(win_hbm.at[:, :, pl.ds(t * 128, 128)], win_raw.at[t], w_sem.at[4 + PARTS + t])
        for t in range(win_raw.shape[0])
    ]
    wout_copy = pltpu.make_async_copy(wout_hbm, wout, w_sem.at[1])
    q_copy = pltpu.make_async_copy(q_hbm, q_ref, w_sem.at[2])
    prompt_copy = pltpu.make_async_copy(prompt_hbm, prompt_raw, w_sem.at[3])
    piece_copies = [
        pltpu.make_async_copy(cache_ref.at[:, h, e], piece_buf[h].at[e], w_sem.at[4 + h])
        for h in range(PARTS)
    ]

    barrier = pltpu.get_barrier_semaphore()
    for k in range(1, ep_count):
        pl.semaphore_signal(barrier, inc=1, device_id=(r, flip(e, k)), device_id_type=MESH)
    pl.semaphore_signal(barrier, inc=1, device_id=(r + ystep, e), device_id_type=MESH)
    for copy in (*win_copies, prompt_copy, wout_copy, q_copy, *piece_copies):
        copy.start()

    for p in range(per_dev):
        tok_f[2 * p : 2 * p + 2] = tok_in[p].astype(jnp.float32)
        top_i[2 * p : 2 * p + 2] = routes_ref[r, p]
        top_f[2 * p : 2 * p + 2] = gates_ref[r, p]
    values = tok_f[...]
    scale = lax.rsqrt(jnp.mean(values * values, axis=-1, keepdims=True) + 1e-06)
    rows_buf[0, :, :width] = (values * scale * gain_ref[...]).astype(jnp.bfloat16)
    lane = lax.broadcasted_iota(jnp.int32, (blk, rows_buf.shape[2] - width), 1)
    dense = jnp.zeros(lane.shape, jnp.float32)
    for k in range(top_i.shape[1]):
        dense += jnp.where(lane % ep_count == top_i[:, k : k + 1], top_f[:, k : k + 1], 0.0)
    high = dense.astype(jnp.bfloat16).astype(jnp.float32)
    tail = jnp.where(lane < ep_count, high, jnp.where(lane < 2 * ep_count, dense - high, 0.0))
    rows_buf[0, :, width:] = tail.astype(jnp.bfloat16)

    pl.semaphore_wait(barrier, ep_count)

    sent = []

    def gather_send(src_slot, dst_slot, dev):
        copy = remote(
            rows_buf.at[src_slot], rows_buf.at[dst_slot], ag_send.at[len(sent)], ag_recv.at[dst_slot], dev
        )
        copy.start()
        sent.append(copy)

    def gather_wait(slot):
        remote(rows_buf.at[0], rows_buf.at[slot], ag_send.at[0], ag_recv.at[slot], partner).wait_recv()

    def spread_own(k):
        if k:
            gather_wait(8 * k)
        gather_send(8 * k, 8 * k + 1, f_dev)
        gather_send(8 * k, 8 * k + 2, g_dev)
        gather_send(8 * k, 8 * k + 4, partner)

    def spread_f(k):
        gather_wait(8 * k + 1)
        gather_send(8 * k + 1, 8 * k + 3, g_dev)
        gather_send(8 * k + 1, 8 * k + 5, partner)

    def spread_g(k):
        for slot in (2, 3):
            gather_wait(8 * k + slot)
            gather_send(8 * k + slot, 8 * k + slot + 4, partner)

    for dz in range(1, nz):
        gather_send(0, 8 * dz, z_dev(dz))
    spread_own(0)

    anc_copies = []
    for k in range(1, ep_count):
        to = (r, flip(e, k))
        anc_copies.append(remote(anc_ref, anc_buf.at[e], anc_send.at[k], anc_recv.at[k], to))
        anc_copies[-1].start()

    first_copies = [[] for _ in range(PARTS)]
    second_copies = [[] for _ in range(PARTS)]

    def peers(at):
        h, dz = at // nz, nz - 1 - at % nz
        return h, [4 * dz + low for low in (3, 2, 1, 0) if 4 * dz + low]

    def first_exchange(at):
        h, masks = peers(at)
        for k in masks:
            peer = flip(e, k)
            at = h * ep_count + k
            first_copies[h].append(
                remote(cache_ref.at[:, h, peer], piece_buf[h].at[e], c1_send.at[at], c1_recv.at[at], (r, peer))
            )
            first_copies[h][-1].start()

    def choose_pieces(h):
        if h == 0:
            anc_buf[pl.ds(e, 1)] = anc_ref[...][None]
            for copy in anc_copies:
                copy.wait()
            anc_local = pltpu.make_async_copy(anc_buf, anc_smem, w_sem.at[0])
            anc_local.start()
            anc_local.wait()
        for copy in first_copies[h]:
            copy.wait_recv()
        piece_copies[h].wait()
        flat = piece_buf[h].reshape(per_dev * ep_count, *piece_buf[h].shape[2:])

        def choose(to, carry):
            for p in range(per_dev):
                chosen[h, to, p] = flat[anc_smem[to, 0, p]]
            return carry

        lax.fori_loop(0, ep_count, choose, 0)
        cache_out[:, h, pl.ds(e, 1)] = chosen[h, pl.ds(e, 1)].reshape(per_dev, 1, *chosen.shape[3:])

    def second_exchange(at):
        h, masks = peers(at)
        for k in masks:
            peer = flip(e, k)
            at = h * ep_count + k
            second_copies[h].append(
                remote(chosen.at[h, peer], cache_out.at[:, h, e], c2_send.at[at], c2_recv.at[at], (r, peer))
            )
            second_copies[h][-1].start()

    def pick_rows(into, kv):
        count = into.shape[1]
        for at in range(kv):
            into[at] = wide[pl.ds(at, count, stride=kv), :].astype(jnp.bfloat16)

    def place_prompt():
        wide[: new_ref.shape[0]] = new_ref[...].astype(jnp.float32)
        pick_rows(own_ref, kv_rows)
        prompt_copy.wait()
        wide[: prompt_raw.shape[0]] = prompt_raw[...].astype(jnp.float32)
        pick_rows(prompt_ref, kv_rows)

    def place_weights(t):
        win_copies[t].wait()
        wide[: 2 * width] = win_raw.at[t].reshape(2 * width, 128)[...].astype(jnp.float32)
        for g in range(2):
            win[:, g * hid + t * 128 : g * hid + (t + 1) * 128] = wide[pl.ds(g, width, stride=2), :].astype(
                jnp.bfloat16
            )

    stages = {}
    rs_at = [0]

    def reduce_send(name, src, dst, dev):
        copy = remote(src, dst, rs_send.at[rs_at[0]], rs_recv.at[rs_at[0]], dev)
        rs_at[0] += 1
        copy.start()
        stages[name] = copy

    def experts(k):
        for slot in range(4, 8):
            gather_wait(8 * k + slot)
        if k == 0:
            wout_copy.wait()
        normed = rows_buf[8 * k : 8 * k + 8, :, :width].reshape(8 * blk, width)
        gate_up = jnp.dot(normed, win[...], preferred_element_type=jnp.float32)
        tail = rows_buf[8 * k : 8 * k + 8, :, width:].astype(jnp.float32).reshape(8 * blk, -1)
        lane = lax.broadcasted_iota(jnp.int32, tail.shape, 1)
        mine = (lane == e) | (lane == e + ep_count)
        gates = jnp.sum(jnp.where(mine, tail, 0.0), axis=-1, keepdims=True)
        value = gate_up[:, :hid]
        act = (value * jax.nn.sigmoid(value) * gate_up[:, hid:] * gates).astype(jnp.bfloat16)
        part[k] = jnp.dot(act, wout[...], preferred_element_type=jnp.float32).astype(jnp.bfloat16)
        reduce_send(("a", k), part.at[k, pl.ds(4 * blk, 4 * blk)], ra.at[k], partner)

    def add_in(k, lo, hi, incoming):
        total = part[k, lo:hi].astype(jnp.float32) + incoming[k, lo:hi].astype(jnp.float32)
        part[k, lo:hi] = total.astype(jnp.bfloat16)

    def reduce_g(k):
        stages["a", k].wait_recv()
        add_in(k, 2 * blk, 4 * blk, ra)
        reduce_send(("b1", k), part.at[k, pl.ds(2 * blk, 2 * blk)], rb1.at[k], g_dev)
        add_in(k, 0, 2 * blk, ra)

    def reduce_f(k):
        stages["b1", k].wait_recv()
        add_in(k, blk, 2 * blk, rb1)
        reduce_send(("b2", k), part.at[k, pl.ds(blk, blk)], rb2.at[k], f_dev)
        add_in(k, 0, blk, rb1)

    def reduce_z(k):
        stages["b2", k].wait_recv()
        add_in(k, 0, blk, rb2)
        if k:
            reduce_send(("z", k), part.at[k, pl.ds(0, blk)], rc.at[k], z_dev(k))

    def reduce_end():
        total = part[0, :blk].astype(jnp.float32)
        for k in range(1, nz):
            stages["z", k].wait_recv()
            total = total + rc[k].astype(jnp.float32)
        exp_out[...] = total

    per_kv = heads[0] // kvh
    q_rows = per_dev * 2 * per_kv
    q_at = lax.broadcasted_iota(jnp.int32, (q_rows, 1), 0)
    q_part = q_at // (2 * per_kv)
    q_pos = (q_at // per_kv) % 2
    new_at = lax.broadcasted_iota(jnp.int32, (1, per_dev * 2), 1)
    new_ok = (new_at // 2 == q_part) & (new_at % 2 <= q_pos)
    gen_len = gen_ref.shape[1] // per_dev
    gen_at = lax.broadcasted_iota(jnp.int32, (1, gen_len * per_dev), 1)
    gen_ok = gen_at // gen_len == q_part
    contract = (((1,), (1,)), ((), ()))

    def attention(n):
        q = q_ref[:, :, n * per_kv : (n + 1) * per_kv, :].reshape(q_rows, hd)
        pairs = [
            (prompt_ref[n], prompt_ref[kvh + n], None),
            (gen_ref[n], gen_ref[kvh + n], gen_ok),
            (own_ref[n], own_ref[kvh + n], new_ok),
        ]
        scores = []
        for key, _, ok in pairs:
            score = lax.dot_general(q, key, contract, preferred_element_type=jnp.float32) * (
                1.0 / math.sqrt(hd)
            )
            scores.append(score if ok is None else jnp.where(ok, score, -jnp.inf))
        top = functools.reduce(jnp.maximum, [s.max(-1, keepdims=True) for s in scores])
        exps = [jnp.exp(s - top) for s in scores]
        inv = 1.0 / functools.reduce(jnp.add, [x.sum(-1, keepdims=True) for x in exps])
        total = 0.0
        for x, (_, value, _) in zip(exps, pairs):
            total = total + jnp.dot(
                (x * inv).astype(jnp.bfloat16), value, preferred_element_type=jnp.float32
            )
        attn_out[:, :, n * per_kv : (n + 1) * per_kv, :] = total.astype(jnp.bfloat16).reshape(
            per_dev, 2, per_kv, hd
        )

    def attend_all():
        for h in range(PARTS):
            for copy in second_copies[h]:
                copy.wait_recv()
        q_copy.wait()
        wide[: gen_ref.shape[1] * kv_rows] = (
            cache_out[...].reshape(gen_ref.shape[1] * kv_rows, hd).astype(jnp.float32)
        )
        pick_rows(gen_ref, kv_rows)
        for n in range(kvh):
            attention(n)

    steps = {
        "O": spread_own,
        "F": spread_f,
        "G": spread_g,
        "X": experts,
        "g": reduce_g,
        "f": reduce_f,
        "z": reduce_z,
        "1": first_exchange,
        "H": choose_pieces,
        "2": second_exchange,
        "P": lambda _: place_prompt(),
        "W": place_weights,
        "A": lambda _: attend_all(),
        "E": lambda _: reduce_end(),
    }
    for name in ORDER:
        steps[name[0]](int(name[1:]))

    for copy in sent:
        copy.wait_send()

    for h in range(PARTS):
        for copy in first_copies[h] + second_copies[h]:
            copy.wait_send()
    for copy in stages.values():
        copy.wait_send()


def place_kernel(cache_ref, attn_ref, experts_ref, cache_out, attn_out, experts_out, sem):
    copies = [
        pltpu.make_async_copy(cache_ref, cache_out, sem.at[0]),
        pltpu.make_async_copy(attn_ref, attn_out, sem.at[1]),
    ]
    for copy in copies:
        copy.start()
    for p in range(experts_out.shape[0]):
        experts_out[p] = experts_ref[2 * p : 2 * p + 2].astype(jnp.bfloat16)
    for copy in copies:
        copy.wait()


def dense_shards(
    gen_cache,
    prompt_cache,
    ancestors,
    queries,
    new_kv,
    tokens_in,
    norm_gain,
    routes,
    gate_weights,
    w_gate_up,
    w_down,
):
    ep_count = lax.axis_size("ep")
    per_dev = gen_cache.shape[0]
    width = tokens_in.shape[2]
    hid = w_down.shape[1]
    heads = (queries.shape[2], new_kv.shape[3])
    hd = queries.shape[3]
    nz = ep_count // 4
    blk = 2 * per_dev
    chunk = 8 * blk
    bf = jnp.bfloat16

    kv_rows = 2 * heads[1]
    top_count = routes.shape[3]
    prompt_len = prompt_cache.shape[0]
    gen_rows = per_dev * gen_cache.shape[1]
    piece_rows = gen_cache.size // (per_dev * PARTS * ep_count * hd)
    tiles = hid // 128
    row = width + -(-2 * ep_count // 128) * 128

    def sems(n):
        return pltpu.SemaphoreType.DMA((n,))

    vmem = pl.BlockSpec(memory_space=pltpu.VMEM)
    hbm = pl.BlockSpec(memory_space=pl.ANY)
    cache_new, attn, experts = pl.pallas_call(
        functools.partial(fused_kernel, ep_count, per_dev, heads),
        out_shape=(
            pltpu.VMEM((per_dev, PARTS, ep_count, piece_rows, hd), bf),
            pltpu.VMEM(queries.shape, bf),
            pltpu.VMEM((blk, width), jnp.float32),
        ),
        in_specs=[vmem] * 6 + [pl.BlockSpec(memory_space=pltpu.HBM)] * 5,
        out_specs=(vmem,) * 3,
        scratch_shapes=[
            pltpu.VMEM((blk, width), jnp.float32),
            pltpu.VMEM((blk, top_count), jnp.int32),
            pltpu.VMEM((blk, top_count), jnp.float32),
            pltpu.VMEM((8 * nz, blk, row), bf),
            pltpu.VMEM((nz, chunk, width), bf),
            pltpu.VMEM((nz, chunk // 2, width), bf),
            pltpu.VMEM((nz, chunk // 4, width), bf),
            pltpu.VMEM((nz, chunk // 8, width), bf),
            pltpu.VMEM((nz, blk, width), bf),
            pltpu.VMEM((ep_count, 1, per_dev), jnp.int32),
            pltpu.SMEM((ep_count, 1, per_dev), jnp.int32),
            (pltpu.VMEM((ep_count, per_dev, piece_rows, hd), bf),) * PARTS,
            pltpu.VMEM((PARTS, ep_count, per_dev, piece_rows, hd), bf),
            pltpu.VMEM((tiles, width, 2, 128), bf),
            pltpu.VMEM((width, 2 * hid), bf),
            pltpu.VMEM((hid, width), bf),
            pltpu.VMEM(queries.shape, bf),
            pltpu.VMEM((prompt_len * kv_rows, hd), bf),
            pltpu.VMEM((max(prompt_len * kv_rows, gen_rows * kv_rows, 2 * width), hd), jnp.float32),
            pltpu.VMEM((kv_rows, prompt_len, hd), bf),
            pltpu.VMEM((kv_rows, gen_rows, hd), bf),
            pltpu.VMEM((kv_rows, blk, hd), bf),
            sems(4 + PARTS + tiles),
            sems(8 * nz),
            sems(8 * nz),
            sems(ep_count),
            sems(ep_count),
            sems(PARTS * ep_count),
            sems(PARTS * ep_count),
            sems(PARTS * ep_count),
            sems(PARTS * ep_count),
            sems(4 * nz),
            sems(4 * nz),
        ],
        compiler_params=pltpu.CompilerParams(collective_id=0, has_side_effects=True, vmem_limit_bytes=40 * 2**20),
        name="resample_attend_experts",
    )(
        *(
            pltpu.with_memory_space_constraint(x, pltpu.HBM)
            for x in (
                tokens_in,
                norm_gain.reshape(1, width),
                routes,
                gate_weights,
                ancestors.reshape(1, per_dev),
                new_kv.reshape(blk * kv_rows, hd),
                gen_cache.reshape(per_dev, PARTS, ep_count, piece_rows, hd),
                queries,
                prompt_cache.reshape(prompt_len * kv_rows, hd),
                w_gate_up.reshape(width, 2, hid),
                w_down.reshape(hid, width),
            )
        ),
    )
    cache_last, attn_last, experts_last = pl.pallas_call(
        place_kernel,
        out_shape=(
            jax.ShapeDtypeStruct(cache_new.shape, bf),
            jax.ShapeDtypeStruct(attn.shape, bf),
            jax.ShapeDtypeStruct(tokens_in.shape, bf),
        ),
        in_specs=[vmem] * 3,
        out_specs=(hbm, hbm, vmem),
        scratch_shapes=[sems(2)],
        name="place_outputs",
    )(*(pltpu.with_memory_space_constraint(x, pltpu.VMEM) for x in (cache_new, attn, experts)))
    return (cache_last.reshape(gen_cache.shape), attn_last, experts_last)


def fits_dense(rep_count, ep_count, per_dev, width, hid):
    if rep_count != 2 or ep_count != 16 or hid % 128:
        return False
    row_bytes = rep_count * ep_count * 2 * per_dev * width * 2
    return 6 * row_bytes + 6 * width * hid < 40 * 2**20


def shards(*args):
    gen_cache, tokens_in, w_down = args[0], args[5], args[10]
    dense = fits_dense(
        lax.axis_size("rep"), lax.axis_size("ep"), gen_cache.shape[0], tokens_in.shape[2], w_down.shape[1]
    )
    return dense_shards(*args) if dense else routed_shards(*args)


def solution(mesh):
    placed = (
        P(("rep", "ep"), None, None, None, None),
        P(),
        P(("rep", "ep")),
        P(("rep", "ep"), None, None, None),
        P(("rep", "ep"), None, None, None, None),
        P(("rep", "ep"), None, None),
        P(),
        P(None, "ep", None, None),
        P(None, "ep", None, None),
        P("ep", None, None, "rep"),
        P("ep", "rep", None),
    )
    return jax.shard_map(
        shards,
        mesh=mesh,
        in_specs=placed,
        out_specs=(
            P(("rep", "ep"), None, None, None, None),
            P(("rep", "ep"), None, None, None),
            P(("rep", "ep"), None, None),
        ),
        check_vma=False,
    )
```

```python
import functools
import math

import jax
import jax.numpy as jnp
from jax import lax
from jax.experimental import pallas as pl
from jax.experimental.pallas import tpu as pltpu
from jax.sharding import PartitionSpec as P

MESH = pl.DeviceIdType.MESH
PARTS = 2
SPLIT = True
ORDER = (
    "10", "11", "12", "13", "14", "15", "16", "17",
    "W0", "F0", "W1", "O1", "O2", "O3", "G0", "W2",
    "F1", "X0", "G1", "F2", "g0", "X1", "G2", "F3",
    "g1", "X2", "f0", "z0", "f1", "G3", "g2", "P0",
    "H0", "20", "21", "22", "23", "X3", "z1", "f2",
    "g3", "H1", "24", "25", "26", "27", "z2", "f3",
    "z3", "A0", "E0",
)


def attend(queries, gen_block, new_block, prompt_cache):
    count = queries.shape[0]
    heads = queries.shape[2]
    head_dim = queries.shape[3]
    kv_heads = new_block.shape[3]
    score_scale = 1.0 / math.sqrt(head_dim)
    grouped = queries.reshape(count, 2, kv_heads, heads // kv_heads, head_dim)
    prompt_scores = (
        jnp.einsum(
            "btngd,snd->btngs", grouped, prompt_cache[:, 0], preferred_element_type=jnp.float32
        )
        * score_scale
    )
    gen_scores = (
        jnp.einsum(
            "btngd,bsnd->btngs", grouped, gen_block[:, :, 0], preferred_element_type=jnp.float32
        )
        * score_scale
    )
    new_scores = (
        jnp.einsum(
            "btngd,bsnd->btngs", grouped, new_block[:, :, 0], preferred_element_type=jnp.float32
        )
        * score_scale
    )
    causal = lax.broadcasted_iota(jnp.int32, (2, 2), 1) <= lax.broadcasted_iota(
        jnp.int32, (2, 2), 0
    )
    new_scores = jnp.where(causal[None, :, None, None, :], new_scores, -jnp.inf)
    row_max = jnp.maximum(
        jnp.maximum(prompt_scores.max(-1), gen_scores.max(-1)), new_scores.max(-1)
    )[..., None]
    prompt_exp = jnp.exp(prompt_scores - row_max)
    gen_exp = jnp.exp(gen_scores - row_max)
    new_exp = jnp.exp(new_scores - row_max)
    denom = (prompt_exp.sum(-1) + gen_exp.sum(-1) + new_exp.sum(-1))[..., None]
    prompt_weights = (prompt_exp / denom).astype(jnp.bfloat16)
    gen_weights = (gen_exp / denom).astype(jnp.bfloat16)
    new_weights = (new_exp / denom).astype(jnp.bfloat16)
    result = jnp.einsum(
        "btngs,snd->btngd", prompt_weights, prompt_cache[:, 1], preferred_element_type=jnp.float32
    )
    result = result + jnp.einsum(
        "btngs,bsnd->btngd", gen_weights, gen_block[:, :, 1], preferred_element_type=jnp.float32
    )
    result = result + jnp.einsum(
        "btngs,bsnd->btngd", new_weights, new_block[:, :, 1], preferred_element_type=jnp.float32
    )
    return result.reshape(count, 2, heads, head_dim).astype(jnp.bfloat16)


def slot_numbers(expert_ids, capacity):
    flat_ids = expert_ids.reshape(-1)
    place = jnp.arange(flat_ids.shape[0], dtype=jnp.int32)
    earlier = place[None, :] < place[:, None]
    same = flat_ids[None, :] == flat_ids[:, None]
    rank = jnp.sum((same & earlier).astype(jnp.int32), axis=1)
    return (flat_ids * capacity + rank).reshape(expert_ids.shape)


def pack_rows(rows, slot_ids, slot_count):
    selector = (
        (jnp.arange(slot_count, dtype=jnp.int32)[:, None, None] == slot_ids[None, :, :])
        .any(-1)
        .astype(jnp.bfloat16)
    )
    return jnp.dot(selector, rows, preferred_element_type=jnp.float32).astype(jnp.bfloat16)


def routed_shards(
    gen_cache,
    prompt_cache,
    ancestors,
    queries,
    new_kv,
    tokens_in,
    norm_gain,
    routes,
    gate_weights,
    w_gate_up,
    w_down,
):
    ep_count = lax.axis_size("ep")
    rep_count = lax.axis_size("rep")
    per_dev = gen_cache.shape[0]
    width = tokens_in.shape[2]
    top_count = routes.shape[3]
    parents = lax.all_gather(ancestors, "ep", axis=0, tiled=True)
    piece_len = gen_cache.size // (per_dev * ep_count)
    flat_cache = gen_cache.reshape(per_dev, ep_count, piece_len)
    chosen = jnp.take(
        lax.all_to_all(flat_cache, "ep", split_axis=1, concat_axis=0, tiled=True), parents, axis=0
    )
    moved = lax.all_to_all(chosen, "ep", split_axis=0, concat_axis=1, tiled=True)
    cache_out = moved.reshape(gen_cache.shape)
    attn_out = attend(queries, cache_out, new_kv, prompt_cache)
    values_f = tokens_in.astype(jnp.float32).reshape(per_dev * 2, width)
    normed = (
        values_f
        * lax.rsqrt(jnp.mean(values_f * values_f, axis=-1, keepdims=True) + 1e-06)
        * norm_gain
    ).astype(jnp.bfloat16)
    half_cols = w_down.shape[1]
    weight_in = w_gate_up.reshape(width, 2 * half_cols)
    weight_out = w_down.reshape(half_cols, width)
    per_expert = min(2 * per_dev, 2 * ((2 * per_dev * top_count + ep_count - 1) // ep_count))
    rep_place = lax.axis_index("rep")
    own_routes = lax.dynamic_index_in_dim(routes, rep_place, 0, keepdims=False).reshape(
        -1, top_count
    )
    own_gates = lax.dynamic_index_in_dim(gate_weights, rep_place, 0, keepdims=False).reshape(
        -1, top_count
    )
    slot_ids = slot_numbers(own_routes, per_expert)
    outgoing = pack_rows(normed, slot_ids, ep_count * per_expert).reshape(
        ep_count, per_expert, width
    )
    received = lax.all_to_all(outgoing, "ep", split_axis=0, concat_axis=0, tiled=True)
    all_rows = lax.all_gather(received, "rep", axis=0, tiled=True)
    gate_up = jnp.dot(all_rows.reshape(-1, width), weight_in, preferred_element_type=jnp.float32)
    act = (jax.nn.silu(gate_up[:, :half_cols]) * gate_up[:, half_cols:]).astype(jnp.bfloat16)
    produced = (
        jnp.dot(act, weight_out, preferred_element_type=jnp.float32)
        .astype(jnp.bfloat16)
        .reshape(all_rows.shape)
    )
    parts_back = lax.all_to_all(produced, "rep", split_axis=0, concat_axis=0, tiled=True)
    added = jnp.sum(parts_back.astype(jnp.float32).reshape((rep_count,) + received.shape), axis=0)
    came_back = (
        lax.all_to_all(added.astype(jnp.bfloat16), "ep", split_axis=0, concat_axis=0, tiled=True)
        .astype(added.dtype)
        .reshape(-1, width)
    )
    picked = jnp.take(came_back, slot_ids, axis=0)
    summed = jnp.sum(own_gates[:, :, None] * picked, axis=1)
    expert_out = summed.astype(jnp.bfloat16).reshape(per_dev, 2, width)
    return (cache_out, attn_out, expert_out)


def flip(value, mask):
    out, bit = value, 1
    while bit <= mask:
        if mask & bit:
            out = out + bit - 2 * bit * ((value // bit) % 2)
        bit *= 2
    return out


def fused_kernel(
    ep_count,
    per_dev,
    heads,
    tok_in,
    gain_ref,
    routes_ref,
    gates_ref,
    anc_ref,
    new_ref,
    cache_ref,
    q_hbm,
    prompt_hbm,
    win_hbm,
    wout_hbm,
    cache_out,
    attn_out,
    exp_out,
    tok_f,
    top_i,
    top_f,
    rows_buf,
    part,
    ra,
    rb1,
    rb2,
    rc,
    anc_buf,
    anc_smem,
    piece_buf,
    chosen,
    win_raw,
    win,
    wout,
    q_ref,
    prompt_raw,
    wide,
    prompt_ref,
    gen_ref,
    own_ref,
    w_sem,
    ag_send,
    ag_recv,
    anc_send,
    anc_recv,
    c1_send,
    c1_recv,
    c2_send,
    c2_recv,
    rs_send,
    rs_recv,
):
    r = lax.axis_index("rep")
    e = lax.axis_index("ep")
    nz = ep_count // 4
    blk = rows_buf.shape[1]
    width = gain_ref.shape[1]
    hid = wout.shape[0]
    hd = q_ref.shape[-1]
    kvh = heads[1]
    kv_rows = 2 * kvh
    c = e % 2
    swap = c if SPLIT else 0
    xstep = 2 - 4 * ((e // 2) % 2)
    ystep = 1 - 2 * r
    f_dev = (r + swap * ystep, e + (1 - swap) * xstep)
    g_dev = (r + (1 - swap) * ystep, e + swap * xstep)
    partner = (r, e + 1 - 2 * c)

    def z_dev(dz):
        return (r, flip(e // 4, dz) * 4 + e % 4)

    def remote(src, dst, ssem, rsem, dev):
        return pltpu.make_async_remote_copy(
            src_ref=src, dst_ref=dst, send_sem=ssem, recv_sem=rsem, device_id=dev, device_id_type=MESH
        )

    win_copies = [
        pltpu.make_async_copy(win_hbm.at[:, :, pl.ds(t * 128, 128)], win_raw.at[t], w_sem.at[4 + PARTS + t])
        for t in range(win_raw.shape[0])
    ]
    wout_copy = pltpu.make_async_copy(wout_hbm, wout, w_sem.at[1])
    q_copy = pltpu.make_async_copy(q_hbm, q_ref, w_sem.at[2])
    prompt_copy = pltpu.make_async_copy(prompt_hbm, prompt_raw, w_sem.at[3])
    piece_copies = [
        pltpu.make_async_copy(cache_ref.at[:, h, e], piece_buf[h].at[e], w_sem.at[4 + h])
        for h in range(PARTS)
    ]

    barrier = pltpu.get_barrier_semaphore()
    for k in range(1, ep_count):
        pl.semaphore_signal(barrier, inc=1, device_id=(r, flip(e, k)), device_id_type=MESH)
    pl.semaphore_signal(barrier, inc=1, device_id=(r + ystep, e), device_id_type=MESH)
    for copy in (*win_copies, prompt_copy, wout_copy, q_copy, *piece_copies):
        copy.start()

    for p in range(per_dev):
        tok_f[2 * p : 2 * p + 2] = tok_in[p].astype(jnp.float32)
        top_i[2 * p : 2 * p + 2] = routes_ref[r, p]
        top_f[2 * p : 2 * p + 2] = gates_ref[r, p]
    values = tok_f[...]
    scale = lax.rsqrt(jnp.mean(values * values, axis=-1, keepdims=True) + 1e-06)
    rows_buf[0, :, :width] = (values * scale * gain_ref[...]).astype(jnp.bfloat16)
    lane = lax.broadcasted_iota(jnp.int32, (blk, rows_buf.shape[2] - width), 1)
    dense = jnp.zeros(lane.shape, jnp.float32)
    for k in range(top_i.shape[1]):
        dense += jnp.where(lane % ep_count == top_i[:, k : k + 1], top_f[:, k : k + 1], 0.0)
    high = dense.astype(jnp.bfloat16).astype(jnp.float32)
    tail = jnp.where(lane < ep_count, high, jnp.where(lane < 2 * ep_count, dense - high, 0.0))
    rows_buf[0, :, width:] = tail.astype(jnp.bfloat16)

    pl.semaphore_wait(barrier, ep_count)

    sent = []

    def gather_send(src_slot, dst_slot, dev):
        copy = remote(
            rows_buf.at[src_slot], rows_buf.at[dst_slot], ag_send.at[len(sent)], ag_recv.at[dst_slot], dev
        )
        copy.start()
        sent.append(copy)

    def gather_wait(slot):
        remote(rows_buf.at[0], rows_buf.at[slot], ag_send.at[0], ag_recv.at[slot], partner).wait_recv()

    def spread_own(k):
        if k:
            gather_wait(8 * k)
        gather_send(8 * k, 8 * k + 1, f_dev)
        gather_send(8 * k, 8 * k + 2, g_dev)
        gather_send(8 * k, 8 * k + 4, partner)

    def spread_f(k):
        gather_wait(8 * k + 1)
        gather_send(8 * k + 1, 8 * k + 3, g_dev)
        gather_send(8 * k + 1, 8 * k + 5, partner)

    def spread_g(k):
        for slot in (2, 3):
            gather_wait(8 * k + slot)
            gather_send(8 * k + slot, 8 * k + slot + 4, partner)

    for dz in range(1, nz):
        gather_send(0, 8 * dz, z_dev(dz))
    spread_own(0)

    anc_copies = []
    for k in range(1, ep_count):
        to = (r, flip(e, k))
        anc_copies.append(remote(anc_ref, anc_buf.at[e], anc_send.at[k], anc_recv.at[k], to))
        anc_copies[-1].start()

    first_copies = [[] for _ in range(PARTS)]
    second_copies = [[] for _ in range(PARTS)]

    def peers(at):
        h, dz = at // nz, nz - 1 - at % nz
        return h, [4 * dz + low for low in (3, 2, 1, 0) if 4 * dz + low]

    def first_exchange(at):
        h, masks = peers(at)
        for k in masks:
            peer = flip(e, k)
            at = h * ep_count + k
            first_copies[h].append(
                remote(cache_ref.at[:, h, peer], piece_buf[h].at[e], c1_send.at[at], c1_recv.at[at], (r, peer))
            )
            first_copies[h][-1].start()

    def choose_pieces(h):
        if h == 0:
            anc_buf[pl.ds(e, 1)] = anc_ref[...][None]
            for copy in anc_copies:
                copy.wait()
            anc_local = pltpu.make_async_copy(anc_buf, anc_smem, w_sem.at[0])
            anc_local.start()
            anc_local.wait()
        for copy in first_copies[h]:
            copy.wait_recv()
        piece_copies[h].wait()
        flat = piece_buf[h].reshape(per_dev * ep_count, *piece_buf[h].shape[2:])

        def choose(to, carry):
            for p in range(per_dev):
                chosen[h, to, p] = flat[anc_smem[to, 0, p]]
            return carry

        lax.fori_loop(0, ep_count, choose, 0)
        cache_out[:, h, pl.ds(e, 1)] = chosen[h, pl.ds(e, 1)].reshape(per_dev, 1, *chosen.shape[3:])

    def second_exchange(at):
        h, masks = peers(at)
        for k in masks:
            peer = flip(e, k)
            at = h * ep_count + k
            second_copies[h].append(
                remote(chosen.at[h, peer], cache_out.at[:, h, e], c2_send.at[at], c2_recv.at[at], (r, peer))
            )
            second_copies[h][-1].start()

    def pick_rows(into, kv):
        count = into.shape[1]
        for at in range(kv):
            into[at] = wide[pl.ds(at, count, stride=kv), :].astype(jnp.bfloat16)

    def place_prompt():
        wide[: new_ref.shape[0]] = new_ref[...].astype(jnp.float32)
        pick_rows(own_ref, kv_rows)
        prompt_copy.wait()
        wide[: prompt_raw.shape[0]] = prompt_raw[...].astype(jnp.float32)
        pick_rows(prompt_ref, kv_rows)

    def place_weights(t):
        win_copies[t].wait()
        wide[: 2 * width] = win_raw.at[t].reshape(2 * width, 128)[...].astype(jnp.float32)
        for g in range(2):
            win[:, g * hid + t * 128 : g * hid + (t + 1) * 128] = wide[pl.ds(g, width, stride=2), :].astype(
                jnp.bfloat16
            )

    stages = {}
    rs_at = [0]

    def reduce_send(name, src, dst, dev):
        copy = remote(src, dst, rs_send.at[rs_at[0]], rs_recv.at[rs_at[0]], dev)
        rs_at[0] += 1
        copy.start()
        stages[name] = copy

    def experts(k):
        for slot in range(4, 8):
            gather_wait(8 * k + slot)
        if k == 0:
            wout_copy.wait()
        normed = rows_buf[8 * k : 8 * k + 8, :, :width].reshape(8 * blk, width)
        gate_up = jnp.dot(normed, win[...], preferred_element_type=jnp.float32)
        tail = rows_buf[8 * k : 8 * k + 8, :, width:].astype(jnp.float32).reshape(8 * blk, -1)
        lane = lax.broadcasted_iota(jnp.int32, tail.shape, 1)
        mine = (lane == e) | (lane == e + ep_count)
        gates = jnp.sum(jnp.where(mine, tail, 0.0), axis=-1, keepdims=True)
        value = gate_up[:, :hid]
        act = (value * jax.nn.sigmoid(value) * gate_up[:, hid:] * gates).astype(jnp.bfloat16)
        part[k] = jnp.dot(act, wout[...], preferred_element_type=jnp.float32).astype(jnp.bfloat16)
        reduce_send(("a", k), part.at[k, pl.ds(4 * blk, 4 * blk)], ra.at[k], partner)

    def add_in(k, lo, hi, incoming):
        total = part[k, lo:hi].astype(jnp.float32) + incoming[k, lo:hi].astype(jnp.float32)
        part[k, lo:hi] = total.astype(jnp.bfloat16)

    def reduce_g(k):
        stages["a", k].wait_recv()
        add_in(k, 2 * blk, 4 * blk, ra)
        reduce_send(("b1", k), part.at[k, pl.ds(2 * blk, 2 * blk)], rb1.at[k], g_dev)
        add_in(k, 0, 2 * blk, ra)

    def reduce_f(k):
        stages["b1", k].wait_recv()
        add_in(k, blk, 2 * blk, rb1)
        reduce_send(("b2", k), part.at[k, pl.ds(blk, blk)], rb2.at[k], f_dev)
        add_in(k, 0, blk, rb1)

    def reduce_z(k):
        stages["b2", k].wait_recv()
        add_in(k, 0, blk, rb2)
        if k:
            reduce_send(("z", k), part.at[k, pl.ds(0, blk)], rc.at[k], z_dev(k))

    def reduce_end():
        total = part[0, :blk].astype(jnp.float32)
        for k in range(1, nz):
            stages["z", k].wait_recv()
            total = total + rc[k].astype(jnp.float32)
        exp_out[...] = total

    per_kv = heads[0] // kvh
    q_rows = per_dev * 2 * per_kv
    q_at = lax.broadcasted_iota(jnp.int32, (q_rows, 1), 0)
    q_part = q_at // (2 * per_kv)
    q_pos = (q_at // per_kv) % 2
    new_at = lax.broadcasted_iota(jnp.int32, (1, per_dev * 2), 1)
    new_ok = (new_at // 2 == q_part) & (new_at % 2 <= q_pos)
    gen_len = gen_ref.shape[1] // per_dev
    gen_at = lax.broadcasted_iota(jnp.int32, (1, gen_len * per_dev), 1)
    gen_ok = gen_at // gen_len == q_part
    contract = (((1,), (1,)), ((), ()))

    def attention(n):
        q = q_ref[:, :, n * per_kv : (n + 1) * per_kv, :].reshape(q_rows, hd)
        pairs = [
            (prompt_ref[n], prompt_ref[kvh + n], None),
            (gen_ref[n], gen_ref[kvh + n], gen_ok),
            (own_ref[n], own_ref[kvh + n], new_ok),
        ]
        scores = []
        for key, _, ok in pairs:
            score = lax.dot_general(q, key, contract, preferred_element_type=jnp.float32) * (
                1.0 / math.sqrt(hd)
            )
            scores.append(score if ok is None else jnp.where(ok, score, -jnp.inf))
        top = functools.reduce(jnp.maximum, [s.max(-1, keepdims=True) for s in scores])
        exps = [jnp.exp(s - top) for s in scores]
        inv = 1.0 / functools.reduce(jnp.add, [x.sum(-1, keepdims=True) for x in exps])
        total = 0.0
        for x, (_, value, _) in zip(exps, pairs):
            total = total + jnp.dot(
                (x * inv).astype(jnp.bfloat16), value, preferred_element_type=jnp.float32
            )
        attn_out[:, :, n * per_kv : (n + 1) * per_kv, :] = total.astype(jnp.bfloat16).reshape(
            per_dev, 2, per_kv, hd
        )

    def attend_all():
        for h in range(PARTS):
            for copy in second_copies[h]:
                copy.wait_recv()
        q_copy.wait()
        wide[: gen_ref.shape[1] * kv_rows] = (
            cache_out[...].reshape(gen_ref.shape[1] * kv_rows, hd).astype(jnp.float32)
        )
        pick_rows(gen_ref, kv_rows)
        for n in range(kvh):
            attention(n)

    steps = {
        "O": spread_own,
        "F": spread_f,
        "G": spread_g,
        "X": experts,
        "g": reduce_g,
        "f": reduce_f,
        "z": reduce_z,
        "1": first_exchange,
        "H": choose_pieces,
        "2": second_exchange,
        "P": lambda _: place_prompt(),
        "W": place_weights,
        "A": lambda _: attend_all(),
        "E": lambda _: reduce_end(),
    }
    for name in ORDER:
        steps[name[0]](int(name[1:]))

    for copy in sent:
        copy.wait_send()

    for h in range(PARTS):
        for copy in first_copies[h] + second_copies[h]:
            copy.wait_send()
    for copy in stages.values():
        copy.wait_send()


def place_kernel(cache_ref, attn_ref, experts_ref, cache_out, attn_out, experts_out, sem):
    copies = [
        pltpu.make_async_copy(cache_ref, cache_out, sem.at[0]),
        pltpu.make_async_copy(attn_ref, attn_out, sem.at[1]),
    ]
    for copy in copies:
        copy.start()
    for p in range(experts_out.shape[0]):
        experts_out[p] = experts_ref[2 * p : 2 * p + 2].astype(jnp.bfloat16)
    for copy in copies:
        copy.wait()


def dense_shards(
    gen_cache,
    prompt_cache,
    ancestors,
    queries,
    new_kv,
    tokens_in,
    norm_gain,
    routes,
    gate_weights,
    w_gate_up,
    w_down,
):
    ep_count = lax.axis_size("ep")
    per_dev = gen_cache.shape[0]
    width = tokens_in.shape[2]
    hid = w_down.shape[1]
    heads = (queries.shape[2], new_kv.shape[3])
    hd = queries.shape[3]
    nz = ep_count // 4
    blk = 2 * per_dev
    chunk = 8 * blk
    bf = jnp.bfloat16

    kv_rows = 2 * heads[1]
    top_count = routes.shape[3]
    prompt_len = prompt_cache.shape[0]
    gen_rows = per_dev * gen_cache.shape[1]
    piece_rows = gen_cache.size // (per_dev * PARTS * ep_count * hd)
    tiles = hid // 128
    row = width + -(-2 * ep_count // 128) * 128

    def sems(n):
        return pltpu.SemaphoreType.DMA((n,))

    vmem = pl.BlockSpec(memory_space=pltpu.VMEM)
    hbm = pl.BlockSpec(memory_space=pl.ANY)
    cache_new, attn, experts = pl.pallas_call(
        functools.partial(fused_kernel, ep_count, per_dev, heads),
        out_shape=(
            pltpu.VMEM((per_dev, PARTS, ep_count, piece_rows, hd), bf),
            pltpu.VMEM(queries.shape, bf),
            pltpu.VMEM((blk, width), jnp.float32),
        ),
        in_specs=[vmem] * 6 + [pl.BlockSpec(memory_space=pltpu.HBM)] * 5,
        out_specs=(vmem,) * 3,
        scratch_shapes=[
            pltpu.VMEM((blk, width), jnp.float32),
            pltpu.VMEM((blk, top_count), jnp.int32),
            pltpu.VMEM((blk, top_count), jnp.float32),
            pltpu.VMEM((8 * nz, blk, row), bf),
            pltpu.VMEM((nz, chunk, width), bf),
            pltpu.VMEM((nz, chunk // 2, width), bf),
            pltpu.VMEM((nz, chunk // 4, width), bf),
            pltpu.VMEM((nz, chunk // 8, width), bf),
            pltpu.VMEM((nz, blk, width), bf),
            pltpu.VMEM((ep_count, 1, per_dev), jnp.int32),
            pltpu.SMEM((ep_count, 1, per_dev), jnp.int32),
            (pltpu.VMEM((ep_count, per_dev, piece_rows, hd), bf),) * PARTS,
            pltpu.VMEM((PARTS, ep_count, per_dev, piece_rows, hd), bf),
            pltpu.VMEM((tiles, width, 2, 128), bf),
            pltpu.VMEM((width, 2 * hid), bf),
            pltpu.VMEM((hid, width), bf),
            pltpu.VMEM(queries.shape, bf),
            pltpu.VMEM((prompt_len * kv_rows, hd), bf),
            pltpu.VMEM((max(prompt_len * kv_rows, gen_rows * kv_rows, 2 * width), hd), jnp.float32),
            pltpu.VMEM((kv_rows, prompt_len, hd), bf),
            pltpu.VMEM((kv_rows, gen_rows, hd), bf),
            pltpu.VMEM((kv_rows, blk, hd), bf),
            sems(4 + PARTS + tiles),
            sems(8 * nz),
            sems(8 * nz),
            sems(ep_count),
            sems(ep_count),
            sems(PARTS * ep_count),
            sems(PARTS * ep_count),
            sems(PARTS * ep_count),
            sems(PARTS * ep_count),
            sems(4 * nz),
            sems(4 * nz),
        ],
        compiler_params=pltpu.CompilerParams(collective_id=0, has_side_effects=True, vmem_limit_bytes=40 * 2**20),
        name="resample_attend_experts",
    )(
        *(
            pltpu.with_memory_space_constraint(x, pltpu.HBM)
            for x in (
                tokens_in,
                norm_gain.reshape(1, width),
                routes,
                gate_weights,
                ancestors.reshape(1, per_dev),
                new_kv.reshape(blk * kv_rows, hd),
                gen_cache.reshape(per_dev, PARTS, ep_count, piece_rows, hd),
                queries,
                prompt_cache.reshape(prompt_len * kv_rows, hd),
                w_gate_up.reshape(width, 2, hid),
                w_down.reshape(hid, width),
            )
        ),
    )
    cache_last, attn_last, experts_last = pl.pallas_call(
        place_kernel,
        out_shape=(
            jax.ShapeDtypeStruct(cache_new.shape, bf),
            jax.ShapeDtypeStruct(attn.shape, bf),
            jax.ShapeDtypeStruct(tokens_in.shape, bf),
        ),
        in_specs=[vmem] * 3,
        out_specs=(hbm, hbm, vmem),
        scratch_shapes=[sems(2)],
        name="place_outputs",
    )(*(pltpu.with_memory_space_constraint(x, pltpu.VMEM) for x in (cache_new, attn, experts)))
    return (cache_last.reshape(gen_cache.shape), attn_last, experts_last)


def fits_dense(rep_count, ep_count, per_dev, width, hid):
    if rep_count != 2 or ep_count != 16 or hid % 128:
        return False
    row_bytes = rep_count * ep_count * 2 * per_dev * width * 2
    return 6 * row_bytes + 6 * width * hid < 40 * 2**20


def shards(*args):
    gen_cache, tokens_in, w_down = args[0], args[5], args[10]
    dense = fits_dense(
        lax.axis_size("rep"), lax.axis_size("ep"), gen_cache.shape[0], tokens_in.shape[2], w_down.shape[1]
    )
    return dense_shards(*args) if dense else routed_shards(*args)


def solution(mesh):
    placed = (
        P(("rep", "ep"), None, None, None, None),
        P(),
        P(("rep", "ep")),
        P(("rep", "ep"), None, None, None),
        P(("rep", "ep"), None, None, None, None),
        P(("rep", "ep"), None, None),
        P(),
        P(None, "ep", None, None),
        P(None, "ep", None, None),
        P("ep", None, None, "rep"),
        P("ep", "rep", None),
    )
    return jax.shard_map(
        shards,
        mesh=mesh,
        in_specs=placed,
        out_specs=(
            P(("rep", "ep"), None, None, None, None),
            P(("rep", "ep"), None, None, None),
            P(("rep", "ep"), None, None),
        ),
        check_vma=False,
    )
```

```python
import functools
import math

import jax
import jax.numpy as jnp
from jax import lax
from jax.experimental import pallas as pl
from jax.experimental.pallas import tpu as pltpu
from jax.sharding import PartitionSpec as P

MESH = pl.DeviceIdType.MESH
PARTS = 2
SPLIT = False
ORDER = (
    "13", "W0", "F0", "W2", "O1", "14", "O2", "G0",
    "16", "11", "O3", "W1", "F1", "X0", "12", "10",
    "F2", "G1", "X1", "15", "G2", "F3", "g1", "17",
    "g0", "H0", "G3", "23", "21", "P0", "H1", "24",
    "22", "X2", "f1", "g2", "20", "26", "X3", "g3",
    "25", "f2", "f3", "z2", "f0", "27", "z3", "z1",
    "z0", "A0", "E0",
)


def attend(queries, gen_block, new_block, prompt_cache):
    count = queries.shape[0]
    heads = queries.shape[2]
    head_dim = queries.shape[3]
    kv_heads = new_block.shape[3]
    score_scale = 1.0 / math.sqrt(head_dim)
    grouped = queries.reshape(count, 2, kv_heads, heads // kv_heads, head_dim)
    prompt_scores = (
        jnp.einsum(
            "btngd,snd->btngs", grouped, prompt_cache[:, 0], preferred_element_type=jnp.float32
        )
        * score_scale
    )
    gen_scores = (
        jnp.einsum(
            "btngd,bsnd->btngs", grouped, gen_block[:, :, 0], preferred_element_type=jnp.float32
        )
        * score_scale
    )
    new_scores = (
        jnp.einsum(
            "btngd,bsnd->btngs", grouped, new_block[:, :, 0], preferred_element_type=jnp.float32
        )
        * score_scale
    )
    causal = lax.broadcasted_iota(jnp.int32, (2, 2), 1) <= lax.broadcasted_iota(
        jnp.int32, (2, 2), 0
    )
    new_scores = jnp.where(causal[None, :, None, None, :], new_scores, -jnp.inf)
    row_max = jnp.maximum(
        jnp.maximum(prompt_scores.max(-1), gen_scores.max(-1)), new_scores.max(-1)
    )[..., None]
    prompt_exp = jnp.exp(prompt_scores - row_max)
    gen_exp = jnp.exp(gen_scores - row_max)
    new_exp = jnp.exp(new_scores - row_max)
    denom = (prompt_exp.sum(-1) + gen_exp.sum(-1) + new_exp.sum(-1))[..., None]
    prompt_weights = (prompt_exp / denom).astype(jnp.bfloat16)
    gen_weights = (gen_exp / denom).astype(jnp.bfloat16)
    new_weights = (new_exp / denom).astype(jnp.bfloat16)
    result = jnp.einsum(
        "btngs,snd->btngd", prompt_weights, prompt_cache[:, 1], preferred_element_type=jnp.float32
    )
    result = result + jnp.einsum(
        "btngs,bsnd->btngd", gen_weights, gen_block[:, :, 1], preferred_element_type=jnp.float32
    )
    result = result + jnp.einsum(
        "btngs,bsnd->btngd", new_weights, new_block[:, :, 1], preferred_element_type=jnp.float32
    )
    return result.reshape(count, 2, heads, head_dim).astype(jnp.bfloat16)


def slot_numbers(expert_ids, capacity):
    flat_ids = expert_ids.reshape(-1)
    place = jnp.arange(flat_ids.shape[0], dtype=jnp.int32)
    earlier = place[None, :] < place[:, None]
    same = flat_ids[None, :] == flat_ids[:, None]
    rank = jnp.sum((same & earlier).astype(jnp.int32), axis=1)
    return (flat_ids * capacity + rank).reshape(expert_ids.shape)


def pack_rows(rows, slot_ids, slot_count):
    selector = (
        (jnp.arange(slot_count, dtype=jnp.int32)[:, None, None] == slot_ids[None, :, :])
        .any(-1)
        .astype(jnp.bfloat16)
    )
    return jnp.dot(selector, rows, preferred_element_type=jnp.float32).astype(jnp.bfloat16)


def routed_shards(
    gen_cache,
    prompt_cache,
    ancestors,
    queries,
    new_kv,
    tokens_in,
    norm_gain,
    routes,
    gate_weights,
    w_gate_up,
    w_down,
):
    ep_count = lax.axis_size("ep")
    rep_count = lax.axis_size("rep")
    per_dev = gen_cache.shape[0]
    width = tokens_in.shape[2]
    top_count = routes.shape[3]
    parents = lax.all_gather(ancestors, "ep", axis=0, tiled=True)
    piece_len = gen_cache.size // (per_dev * ep_count)
    flat_cache = gen_cache.reshape(per_dev, ep_count, piece_len)
    chosen = jnp.take(
        lax.all_to_all(flat_cache, "ep", split_axis=1, concat_axis=0, tiled=True), parents, axis=0
    )
    moved = lax.all_to_all(chosen, "ep", split_axis=0, concat_axis=1, tiled=True)
    cache_out = moved.reshape(gen_cache.shape)
    attn_out = attend(queries, cache_out, new_kv, prompt_cache)
    values_f = tokens_in.astype(jnp.float32).reshape(per_dev * 2, width)
    normed = (
        values_f
        * lax.rsqrt(jnp.mean(values_f * values_f, axis=-1, keepdims=True) + 1e-06)
        * norm_gain
    ).astype(jnp.bfloat16)
    half_cols = w_down.shape[1]
    weight_in = w_gate_up.reshape(width, 2 * half_cols)
    weight_out = w_down.reshape(half_cols, width)
    per_expert = min(2 * per_dev, 2 * ((2 * per_dev * top_count + ep_count - 1) // ep_count))
    rep_place = lax.axis_index("rep")
    own_routes = lax.dynamic_index_in_dim(routes, rep_place, 0, keepdims=False).reshape(
        -1, top_count
    )
    own_gates = lax.dynamic_index_in_dim(gate_weights, rep_place, 0, keepdims=False).reshape(
        -1, top_count
    )
    slot_ids = slot_numbers(own_routes, per_expert)
    outgoing = pack_rows(normed, slot_ids, ep_count * per_expert).reshape(
        ep_count, per_expert, width
    )
    received = lax.all_to_all(outgoing, "ep", split_axis=0, concat_axis=0, tiled=True)
    all_rows = lax.all_gather(received, "rep", axis=0, tiled=True)
    gate_up = jnp.dot(all_rows.reshape(-1, width), weight_in, preferred_element_type=jnp.float32)
    act = (jax.nn.silu(gate_up[:, :half_cols]) * gate_up[:, half_cols:]).astype(jnp.bfloat16)
    produced = (
        jnp.dot(act, weight_out, preferred_element_type=jnp.float32)
        .astype(jnp.bfloat16)
        .reshape(all_rows.shape)
    )
    parts_back = lax.all_to_all(produced, "rep", split_axis=0, concat_axis=0, tiled=True)
    added = jnp.sum(parts_back.astype(jnp.float32).reshape((rep_count,) + received.shape), axis=0)
    came_back = (
        lax.all_to_all(added.astype(jnp.bfloat16), "ep", split_axis=0, concat_axis=0, tiled=True)
        .astype(added.dtype)
        .reshape(-1, width)
    )
    picked = jnp.take(came_back, slot_ids, axis=0)
    summed = jnp.sum(own_gates[:, :, None] * picked, axis=1)
    expert_out = summed.astype(jnp.bfloat16).reshape(per_dev, 2, width)
    return (cache_out, attn_out, expert_out)


def flip(value, mask):
    out, bit = value, 1
    while bit <= mask:
        if mask & bit:
            out = out + bit - 2 * bit * ((value // bit) % 2)
        bit *= 2
    return out


def fused_kernel(
    ep_count,
    per_dev,
    heads,
    tok_in,
    gain_ref,
    routes_ref,
    gates_ref,
    anc_ref,
    new_ref,
    cache_ref,
    q_hbm,
    prompt_hbm,
    win_hbm,
    wout_hbm,
    cache_out,
    attn_out,
    exp_out,
    tok_f,
    top_i,
    top_f,
    rows_buf,
    part,
    ra,
    rb1,
    rb2,
    rc,
    anc_buf,
    anc_smem,
    piece_buf,
    chosen,
    win_raw,
    win,
    wout,
    q_ref,
    prompt_raw,
    wide,
    prompt_ref,
    gen_ref,
    own_ref,
    w_sem,
    ag_send,
    ag_recv,
    anc_send,
    anc_recv,
    c1_send,
    c1_recv,
    c2_send,
    c2_recv,
    rs_send,
    rs_recv,
):
    r = lax.axis_index("rep")
    e = lax.axis_index("ep")
    nz = ep_count // 4
    blk = rows_buf.shape[1]
    width = gain_ref.shape[1]
    hid = wout.shape[0]
    hd = q_ref.shape[-1]
    kvh = heads[1]
    kv_rows = 2 * kvh
    c = e % 2
    swap = c if SPLIT else 0
    xstep = 2 - 4 * ((e // 2) % 2)
    ystep = 1 - 2 * r
    f_dev = (r + swap * ystep, e + (1 - swap) * xstep)
    g_dev = (r + (1 - swap) * ystep, e + swap * xstep)
    partner = (r, e + 1 - 2 * c)

    def z_dev(dz):
        return (r, flip(e // 4, dz) * 4 + e % 4)

    def remote(src, dst, ssem, rsem, dev):
        return pltpu.make_async_remote_copy(
            src_ref=src, dst_ref=dst, send_sem=ssem, recv_sem=rsem, device_id=dev, device_id_type=MESH
        )

    win_copies = [
        pltpu.make_async_copy(win_hbm.at[:, :, pl.ds(t * 128, 128)], win_raw.at[t], w_sem.at[4 + PARTS + t])
        for t in range(win_raw.shape[0])
    ]
    wout_copy = pltpu.make_async_copy(wout_hbm, wout, w_sem.at[1])
    q_copy = pltpu.make_async_copy(q_hbm, q_ref, w_sem.at[2])
    prompt_copy = pltpu.make_async_copy(prompt_hbm, prompt_raw, w_sem.at[3])
    piece_copies = [
        pltpu.make_async_copy(cache_ref.at[:, h, e], piece_buf[h].at[e], w_sem.at[4 + h])
        for h in range(PARTS)
    ]

    barrier = pltpu.get_barrier_semaphore()
    for k in range(1, ep_count):
        pl.semaphore_signal(barrier, inc=1, device_id=(r, flip(e, k)), device_id_type=MESH)
    pl.semaphore_signal(barrier, inc=1, device_id=(r + ystep, e), device_id_type=MESH)
    for copy in (*win_copies, prompt_copy, wout_copy, q_copy, *piece_copies):
        copy.start()

    for p in range(per_dev):
        tok_f[2 * p : 2 * p + 2] = tok_in[p].astype(jnp.float32)
        top_i[2 * p : 2 * p + 2] = routes_ref[r, p]
        top_f[2 * p : 2 * p + 2] = gates_ref[r, p]
    values = tok_f[...]
    scale = lax.rsqrt(jnp.mean(values * values, axis=-1, keepdims=True) + 1e-06)
    rows_buf[0, :, :width] = (values * scale * gain_ref[...]).astype(jnp.bfloat16)
    lane = lax.broadcasted_iota(jnp.int32, (blk, rows_buf.shape[2] - width), 1)
    dense = jnp.zeros(lane.shape, jnp.float32)
    for k in range(top_i.shape[1]):
        dense += jnp.where(lane % ep_count == top_i[:, k : k + 1], top_f[:, k : k + 1], 0.0)
    high = dense.astype(jnp.bfloat16).astype(jnp.float32)
    tail = jnp.where(lane < ep_count, high, jnp.where(lane < 2 * ep_count, dense - high, 0.0))
    rows_buf[0, :, width:] = tail.astype(jnp.bfloat16)

    pl.semaphore_wait(barrier, ep_count)

    sent = []

    def gather_send(src_slot, dst_slot, dev):
        copy = remote(
            rows_buf.at[src_slot], rows_buf.at[dst_slot], ag_send.at[len(sent)], ag_recv.at[dst_slot], dev
        )
        copy.start()
        sent.append(copy)

    def gather_wait(slot):
        remote(rows_buf.at[0], rows_buf.at[slot], ag_send.at[0], ag_recv.at[slot], partner).wait_recv()

    def spread_own(k):
        if k:
            gather_wait(8 * k)
        gather_send(8 * k, 8 * k + 1, f_dev)
        gather_send(8 * k, 8 * k + 2, g_dev)
        gather_send(8 * k, 8 * k + 4, partner)

    def spread_f(k):
        gather_wait(8 * k + 1)
        gather_send(8 * k + 1, 8 * k + 3, g_dev)
        gather_send(8 * k + 1, 8 * k + 5, partner)

    def spread_g(k):
        for slot in (2, 3):
            gather_wait(8 * k + slot)
            gather_send(8 * k + slot, 8 * k + slot + 4, partner)

    for dz in range(1, nz):
        gather_send(0, 8 * dz, z_dev(dz))
    spread_own(0)

    anc_copies = []
    for k in range(1, ep_count):
        to = (r, flip(e, k))
        anc_copies.append(remote(anc_ref, anc_buf.at[e], anc_send.at[k], anc_recv.at[k], to))
        anc_copies[-1].start()

    first_copies = [[] for _ in range(PARTS)]
    second_copies = [[] for _ in range(PARTS)]

    def peers(at):
        h, dz = at // nz, nz - 1 - at % nz
        return h, [4 * dz + low for low in (3, 2, 1, 0) if 4 * dz + low]

    def first_exchange(at):
        h, masks = peers(at)
        for k in masks:
            peer = flip(e, k)
            at = h * ep_count + k
            first_copies[h].append(
                remote(cache_ref.at[:, h, peer], piece_buf[h].at[e], c1_send.at[at], c1_recv.at[at], (r, peer))
            )
            first_copies[h][-1].start()

    def choose_pieces(h):
        if h == 0:
            anc_buf[pl.ds(e, 1)] = anc_ref[...][None]
            for copy in anc_copies:
                copy.wait()
            anc_local = pltpu.make_async_copy(anc_buf, anc_smem, w_sem.at[0])
            anc_local.start()
            anc_local.wait()
        for copy in first_copies[h]:
            copy.wait_recv()
        piece_copies[h].wait()
        flat = piece_buf[h].reshape(per_dev * ep_count, *piece_buf[h].shape[2:])

        def choose(to, carry):
            for p in range(per_dev):
                chosen[h, to, p] = flat[anc_smem[to, 0, p]]
            return carry

        lax.fori_loop(0, ep_count, choose, 0)
        cache_out[:, h, pl.ds(e, 1)] = chosen[h, pl.ds(e, 1)].reshape(per_dev, 1, *chosen.shape[3:])

    def second_exchange(at):
        h, masks = peers(at)
        for k in masks:
            peer = flip(e, k)
            at = h * ep_count + k
            second_copies[h].append(
                remote(chosen.at[h, peer], cache_out.at[:, h, e], c2_send.at[at], c2_recv.at[at], (r, peer))
            )
            second_copies[h][-1].start()

    def pick_rows(into, kv):
        count = into.shape[1]
        for at in range(kv):
            into[at] = wide[pl.ds(at, count, stride=kv), :].astype(jnp.bfloat16)

    def place_prompt():
        wide[: new_ref.shape[0]] = new_ref[...].astype(jnp.float32)
        pick_rows(own_ref, kv_rows)
        prompt_copy.wait()
        wide[: prompt_raw.shape[0]] = prompt_raw[...].astype(jnp.float32)
        pick_rows(prompt_ref, kv_rows)

    def place_weights(t):
        win_copies[t].wait()
        wide[: 2 * width] = win_raw.at[t].reshape(2 * width, 128)[...].astype(jnp.float32)
        for g in range(2):
            win[:, g * hid + t * 128 : g * hid + (t + 1) * 128] = wide[pl.ds(g, width, stride=2), :].astype(
                jnp.bfloat16
            )

    stages = {}
    rs_at = [0]

    def reduce_send(name, src, dst, dev):
        copy = remote(src, dst, rs_send.at[rs_at[0]], rs_recv.at[rs_at[0]], dev)
        rs_at[0] += 1
        copy.start()
        stages[name] = copy

    def experts(k):
        for slot in range(4, 8):
            gather_wait(8 * k + slot)
        if k == 0:
            wout_copy.wait()
        normed = rows_buf[8 * k : 8 * k + 8, :, :width].reshape(8 * blk, width)
        gate_up = jnp.dot(normed, win[...], preferred_element_type=jnp.float32)
        tail = rows_buf[8 * k : 8 * k + 8, :, width:].astype(jnp.float32).reshape(8 * blk, -1)
        lane = lax.broadcasted_iota(jnp.int32, tail.shape, 1)
        mine = (lane == e) | (lane == e + ep_count)
        gates = jnp.sum(jnp.where(mine, tail, 0.0), axis=-1, keepdims=True)
        value = gate_up[:, :hid]
        act = (value * jax.nn.sigmoid(value) * gate_up[:, hid:] * gates).astype(jnp.bfloat16)
        part[k] = jnp.dot(act, wout[...], preferred_element_type=jnp.float32).astype(jnp.bfloat16)
        reduce_send(("a", k), part.at[k, pl.ds(4 * blk, 4 * blk)], ra.at[k], partner)

    def add_in(k, lo, hi, incoming):
        total = part[k, lo:hi].astype(jnp.float32) + incoming[k, lo:hi].astype(jnp.float32)
        part[k, lo:hi] = total.astype(jnp.bfloat16)

    def reduce_g(k):
        stages["a", k].wait_recv()
        add_in(k, 2 * blk, 4 * blk, ra)
        reduce_send(("b1", k), part.at[k, pl.ds(2 * blk, 2 * blk)], rb1.at[k], g_dev)
        add_in(k, 0, 2 * blk, ra)

    def reduce_f(k):
        stages["b1", k].wait_recv()
        add_in(k, blk, 2 * blk, rb1)
        reduce_send(("b2", k), part.at[k, pl.ds(blk, blk)], rb2.at[k], f_dev)
        add_in(k, 0, blk, rb1)

    def reduce_z(k):
        stages["b2", k].wait_recv()
        add_in(k, 0, blk, rb2)
        if k:
            reduce_send(("z", k), part.at[k, pl.ds(0, blk)], rc.at[k], z_dev(k))

    def reduce_end():
        total = part[0, :blk].astype(jnp.float32)
        for k in range(1, nz):
            stages["z", k].wait_recv()
            total = total + rc[k].astype(jnp.float32)
        exp_out[...] = total

    per_kv = heads[0] // kvh
    q_rows = per_dev * 2 * per_kv
    q_at = lax.broadcasted_iota(jnp.int32, (q_rows, 1), 0)
    q_part = q_at // (2 * per_kv)
    q_pos = (q_at // per_kv) % 2
    new_at = lax.broadcasted_iota(jnp.int32, (1, per_dev * 2), 1)
    new_ok = (new_at // 2 == q_part) & (new_at % 2 <= q_pos)
    gen_len = gen_ref.shape[1] // per_dev
    gen_at = lax.broadcasted_iota(jnp.int32, (1, gen_len * per_dev), 1)
    gen_ok = gen_at // gen_len == q_part
    contract = (((1,), (1,)), ((), ()))

    def attention(n):
        q = q_ref[:, :, n * per_kv : (n + 1) * per_kv, :].reshape(q_rows, hd)
        pairs = [
            (prompt_ref[n], prompt_ref[kvh + n], None),
            (gen_ref[n], gen_ref[kvh + n], gen_ok),
            (own_ref[n], own_ref[kvh + n], new_ok),
        ]
        scores = []
        for key, _, ok in pairs:
            score = lax.dot_general(q, key, contract, preferred_element_type=jnp.float32) * (
                1.0 / math.sqrt(hd)
            )
            scores.append(score if ok is None else jnp.where(ok, score, -jnp.inf))
        top = functools.reduce(jnp.maximum, [s.max(-1, keepdims=True) for s in scores])
        exps = [jnp.exp(s - top) for s in scores]
        inv = 1.0 / functools.reduce(jnp.add, [x.sum(-1, keepdims=True) for x in exps])
        total = 0.0
        for x, (_, value, _) in zip(exps, pairs):
            total = total + jnp.dot(
                (x * inv).astype(jnp.bfloat16), value, preferred_element_type=jnp.float32
            )
        attn_out[:, :, n * per_kv : (n + 1) * per_kv, :] = total.astype(jnp.bfloat16).reshape(
            per_dev, 2, per_kv, hd
        )

    def attend_all():
        for h in range(PARTS):
            for copy in second_copies[h]:
                copy.wait_recv()
        q_copy.wait()
        wide[: gen_ref.shape[1] * kv_rows] = (
            cache_out[...].reshape(gen_ref.shape[1] * kv_rows, hd).astype(jnp.float32)
        )
        pick_rows(gen_ref, kv_rows)
        for n in range(kvh):
            attention(n)

    steps = {
        "O": spread_own,
        "F": spread_f,
        "G": spread_g,
        "X": experts,
        "g": reduce_g,
        "f": reduce_f,
        "z": reduce_z,
        "1": first_exchange,
        "H": choose_pieces,
        "2": second_exchange,
        "P": lambda _: place_prompt(),
        "W": place_weights,
        "A": lambda _: attend_all(),
        "E": lambda _: reduce_end(),
    }
    for name in ORDER:
        steps[name[0]](int(name[1:]))

    for copy in sent:
        copy.wait_send()

    for h in range(PARTS):
        for copy in first_copies[h] + second_copies[h]:
            copy.wait_send()
    for copy in stages.values():
        copy.wait_send()


def place_kernel(cache_ref, attn_ref, experts_ref, cache_out, attn_out, experts_out, sem):
    copies = [
        pltpu.make_async_copy(cache_ref, cache_out, sem.at[0]),
        pltpu.make_async_copy(attn_ref, attn_out, sem.at[1]),
    ]
    for copy in copies:
        copy.start()
    for p in range(experts_out.shape[0]):
        experts_out[p] = experts_ref[2 * p : 2 * p + 2].astype(jnp.bfloat16)
    for copy in copies:
        copy.wait()


def dense_shards(
    gen_cache,
    prompt_cache,
    ancestors,
    queries,
    new_kv,
    tokens_in,
    norm_gain,
    routes,
    gate_weights,
    w_gate_up,
    w_down,
):
    ep_count = lax.axis_size("ep")
    per_dev = gen_cache.shape[0]
    width = tokens_in.shape[2]
    hid = w_down.shape[1]
    heads = (queries.shape[2], new_kv.shape[3])
    hd = queries.shape[3]
    nz = ep_count // 4
    blk = 2 * per_dev
    chunk = 8 * blk
    bf = jnp.bfloat16

    kv_rows = 2 * heads[1]
    top_count = routes.shape[3]
    prompt_len = prompt_cache.shape[0]
    gen_rows = per_dev * gen_cache.shape[1]
    piece_rows = gen_cache.size // (per_dev * PARTS * ep_count * hd)
    tiles = hid // 128
    row = width + -(-2 * ep_count // 128) * 128

    def sems(n):
        return pltpu.SemaphoreType.DMA((n,))

    vmem = pl.BlockSpec(memory_space=pltpu.VMEM)
    hbm = pl.BlockSpec(memory_space=pl.ANY)
    cache_new, attn, experts = pl.pallas_call(
        functools.partial(fused_kernel, ep_count, per_dev, heads),
        out_shape=(
            pltpu.VMEM((per_dev, PARTS, ep_count, piece_rows, hd), bf),
            pltpu.VMEM(queries.shape, bf),
            pltpu.VMEM((blk, width), jnp.float32),
        ),
        in_specs=[vmem] * 6 + [pl.BlockSpec(memory_space=pltpu.HBM)] * 5,
        out_specs=(vmem,) * 3,
        scratch_shapes=[
            pltpu.VMEM((blk, width), jnp.float32),
            pltpu.VMEM((blk, top_count), jnp.int32),
            pltpu.VMEM((blk, top_count), jnp.float32),
            pltpu.VMEM((8 * nz, blk, row), bf),
            pltpu.VMEM((nz, chunk, width), bf),
            pltpu.VMEM((nz, chunk // 2, width), bf),
            pltpu.VMEM((nz, chunk // 4, width), bf),
            pltpu.VMEM((nz, chunk // 8, width), bf),
            pltpu.VMEM((nz, blk, width), bf),
            pltpu.VMEM((ep_count, 1, per_dev), jnp.int32),
            pltpu.SMEM((ep_count, 1, per_dev), jnp.int32),
            (pltpu.VMEM((ep_count, per_dev, piece_rows, hd), bf),) * PARTS,
            pltpu.VMEM((PARTS, ep_count, per_dev, piece_rows, hd), bf),
            pltpu.VMEM((tiles, width, 2, 128), bf),
            pltpu.VMEM((width, 2 * hid), bf),
            pltpu.VMEM((hid, width), bf),
            pltpu.VMEM(queries.shape, bf),
            pltpu.VMEM((prompt_len * kv_rows, hd), bf),
            pltpu.VMEM((max(prompt_len * kv_rows, gen_rows * kv_rows, 2 * width), hd), jnp.float32),
            pltpu.VMEM((kv_rows, prompt_len, hd), bf),
            pltpu.VMEM((kv_rows, gen_rows, hd), bf),
            pltpu.VMEM((kv_rows, blk, hd), bf),
            sems(4 + PARTS + tiles),
            sems(8 * nz),
            sems(8 * nz),
            sems(ep_count),
            sems(ep_count),
            sems(PARTS * ep_count),
            sems(PARTS * ep_count),
            sems(PARTS * ep_count),
            sems(PARTS * ep_count),
            sems(4 * nz),
            sems(4 * nz),
        ],
        compiler_params=pltpu.CompilerParams(collective_id=0, has_side_effects=True, vmem_limit_bytes=40 * 2**20),
        name="resample_attend_experts",
    )(
        *(
            pltpu.with_memory_space_constraint(x, pltpu.HBM)
            for x in (
                tokens_in,
                norm_gain.reshape(1, width),
                routes,
                gate_weights,
                ancestors.reshape(1, per_dev),
                new_kv.reshape(blk * kv_rows, hd),
                gen_cache.reshape(per_dev, PARTS, ep_count, piece_rows, hd),
                queries,
                prompt_cache.reshape(prompt_len * kv_rows, hd),
                w_gate_up.reshape(width, 2, hid),
                w_down.reshape(hid, width),
            )
        ),
    )
    cache_last, attn_last, experts_last = pl.pallas_call(
        place_kernel,
        out_shape=(
            jax.ShapeDtypeStruct(cache_new.shape, bf),
            jax.ShapeDtypeStruct(attn.shape, bf),
            jax.ShapeDtypeStruct(tokens_in.shape, bf),
        ),
        in_specs=[vmem] * 3,
        out_specs=(hbm, hbm, vmem),
        scratch_shapes=[sems(2)],
        name="place_outputs",
    )(*(pltpu.with_memory_space_constraint(x, pltpu.VMEM) for x in (cache_new, attn, experts)))
    return (cache_last.reshape(gen_cache.shape), attn_last, experts_last)


def fits_dense(rep_count, ep_count, per_dev, width, hid):
    if rep_count != 2 or ep_count != 16 or hid % 128:
        return False
    row_bytes = rep_count * ep_count * 2 * per_dev * width * 2
    return 6 * row_bytes + 6 * width * hid < 40 * 2**20


def shards(*args):
    gen_cache, tokens_in, w_down = args[0], args[5], args[10]
    dense = fits_dense(
        lax.axis_size("rep"), lax.axis_size("ep"), gen_cache.shape[0], tokens_in.shape[2], w_down.shape[1]
    )
    return dense_shards(*args) if dense else routed_shards(*args)


def solution(mesh):
    placed = (
        P(("rep", "ep"), None, None, None, None),
        P(),
        P(("rep", "ep")),
        P(("rep", "ep"), None, None, None),
        P(("rep", "ep"), None, None, None, None),
        P(("rep", "ep"), None, None),
        P(),
        P(None, "ep", None, None),
        P(None, "ep", None, None),
        P("ep", None, None, "rep"),
        P("ep", "rep", None),
    )
    return jax.shard_map(
        shards,
        mesh=mesh,
        in_specs=placed,
        out_specs=(
            P(("rep", "ep"), None, None, None, None),
            P(("rep", "ep"), None, None, None),
            P(("rep", "ep"), None, None),
        ),
        check_vma=False,
    )
```

```python
import functools
import math

import jax
import jax.numpy as jnp
from jax import lax
from jax.experimental import pallas as pl
from jax.experimental.pallas import tpu as pltpu
from jax.sharding import PartitionSpec as P

MESH = pl.DeviceIdType.MESH
PARTS = 2
SPLIT = False
ORDER = (
    "F0", "14", "W2", "O1", "W1", "11", "O2", "F1",
    "W0", "O3", "F2", "10", "12", "G1", "13", "G0",
    "X1", "17", "F3", "15", "16", "g1", "H0", "G2",
    "21", "22", "20", "X2", "H1", "27", "g2", "25",
    "G3", "f1", "X3", "X0", "g3", "26", "g0", "23",
    "f2", "24", "z2", "f3", "P0", "z3", "f0", "z1",
    "A0", "z0", "E0",
)


def attend(queries, gen_block, new_block, prompt_cache):
    count = queries.shape[0]
    heads = queries.shape[2]
    head_dim = queries.shape[3]
    kv_heads = new_block.shape[3]
    score_scale = 1.0 / math.sqrt(head_dim)
    grouped = queries.reshape(count, 2, kv_heads, heads // kv_heads, head_dim)
    prompt_scores = (
        jnp.einsum(
            "btngd,snd->btngs", grouped, prompt_cache[:, 0], preferred_element_type=jnp.float32
        )
        * score_scale
    )
    gen_scores = (
        jnp.einsum(
            "btngd,bsnd->btngs", grouped, gen_block[:, :, 0], preferred_element_type=jnp.float32
        )
        * score_scale
    )
    new_scores = (
        jnp.einsum(
            "btngd,bsnd->btngs", grouped, new_block[:, :, 0], preferred_element_type=jnp.float32
        )
        * score_scale
    )
    causal = lax.broadcasted_iota(jnp.int32, (2, 2), 1) <= lax.broadcasted_iota(
        jnp.int32, (2, 2), 0
    )
    new_scores = jnp.where(causal[None, :, None, None, :], new_scores, -jnp.inf)
    row_max = jnp.maximum(
        jnp.maximum(prompt_scores.max(-1), gen_scores.max(-1)), new_scores.max(-1)
    )[..., None]
    prompt_exp = jnp.exp(prompt_scores - row_max)
    gen_exp = jnp.exp(gen_scores - row_max)
    new_exp = jnp.exp(new_scores - row_max)
    denom = (prompt_exp.sum(-1) + gen_exp.sum(-1) + new_exp.sum(-1))[..., None]
    prompt_weights = (prompt_exp / denom).astype(jnp.bfloat16)
    gen_weights = (gen_exp / denom).astype(jnp.bfloat16)
    new_weights = (new_exp / denom).astype(jnp.bfloat16)
    result = jnp.einsum(
        "btngs,snd->btngd", prompt_weights, prompt_cache[:, 1], preferred_element_type=jnp.float32
    )
    result = result + jnp.einsum(
        "btngs,bsnd->btngd", gen_weights, gen_block[:, :, 1], preferred_element_type=jnp.float32
    )
    result = result + jnp.einsum(
        "btngs,bsnd->btngd", new_weights, new_block[:, :, 1], preferred_element_type=jnp.float32
    )
    return result.reshape(count, 2, heads, head_dim).astype(jnp.bfloat16)


def slot_numbers(expert_ids, capacity):
    flat_ids = expert_ids.reshape(-1)
    place = jnp.arange(flat_ids.shape[0], dtype=jnp.int32)
    earlier = place[None, :] < place[:, None]
    same = flat_ids[None, :] == flat_ids[:, None]
    rank = jnp.sum((same & earlier).astype(jnp.int32), axis=1)
    return (flat_ids * capacity + rank).reshape(expert_ids.shape)


def pack_rows(rows, slot_ids, slot_count):
    selector = (
        (jnp.arange(slot_count, dtype=jnp.int32)[:, None, None] == slot_ids[None, :, :])
        .any(-1)
        .astype(jnp.bfloat16)
    )
    return jnp.dot(selector, rows, preferred_element_type=jnp.float32).astype(jnp.bfloat16)


def routed_shards(
    gen_cache,
    prompt_cache,
    ancestors,
    queries,
    new_kv,
    tokens_in,
    norm_gain,
    routes,
    gate_weights,
    w_gate_up,
    w_down,
):
    ep_count = lax.axis_size("ep")
    rep_count = lax.axis_size("rep")
    per_dev = gen_cache.shape[0]
    width = tokens_in.shape[2]
    top_count = routes.shape[3]
    parents = lax.all_gather(ancestors, "ep", axis=0, tiled=True)
    piece_len = gen_cache.size // (per_dev * ep_count)
    flat_cache = gen_cache.reshape(per_dev, ep_count, piece_len)
    chosen = jnp.take(
        lax.all_to_all(flat_cache, "ep", split_axis=1, concat_axis=0, tiled=True), parents, axis=0
    )
    moved = lax.all_to_all(chosen, "ep", split_axis=0, concat_axis=1, tiled=True)
    cache_out = moved.reshape(gen_cache.shape)
    attn_out = attend(queries, cache_out, new_kv, prompt_cache)
    values_f = tokens_in.astype(jnp.float32).reshape(per_dev * 2, width)
    normed = (
        values_f
        * lax.rsqrt(jnp.mean(values_f * values_f, axis=-1, keepdims=True) + 1e-06)
        * norm_gain
    ).astype(jnp.bfloat16)
    half_cols = w_down.shape[1]
    weight_in = w_gate_up.reshape(width, 2 * half_cols)
    weight_out = w_down.reshape(half_cols, width)
    per_expert = min(2 * per_dev, 2 * ((2 * per_dev * top_count + ep_count - 1) // ep_count))
    rep_place = lax.axis_index("rep")
    own_routes = lax.dynamic_index_in_dim(routes, rep_place, 0, keepdims=False).reshape(
        -1, top_count
    )
    own_gates = lax.dynamic_index_in_dim(gate_weights, rep_place, 0, keepdims=False).reshape(
        -1, top_count
    )
    slot_ids = slot_numbers(own_routes, per_expert)
    outgoing = pack_rows(normed, slot_ids, ep_count * per_expert).reshape(
        ep_count, per_expert, width
    )
    received = lax.all_to_all(outgoing, "ep", split_axis=0, concat_axis=0, tiled=True)
    all_rows = lax.all_gather(received, "rep", axis=0, tiled=True)
    gate_up = jnp.dot(all_rows.reshape(-1, width), weight_in, preferred_element_type=jnp.float32)
    act = (jax.nn.silu(gate_up[:, :half_cols]) * gate_up[:, half_cols:]).astype(jnp.bfloat16)
    produced = (
        jnp.dot(act, weight_out, preferred_element_type=jnp.float32)
        .astype(jnp.bfloat16)
        .reshape(all_rows.shape)
    )
    parts_back = lax.all_to_all(produced, "rep", split_axis=0, concat_axis=0, tiled=True)
    added = jnp.sum(parts_back.astype(jnp.float32).reshape((rep_count,) + received.shape), axis=0)
    came_back = (
        lax.all_to_all(added.astype(jnp.bfloat16), "ep", split_axis=0, concat_axis=0, tiled=True)
        .astype(added.dtype)
        .reshape(-1, width)
    )
    picked = jnp.take(came_back, slot_ids, axis=0)
    summed = jnp.sum(own_gates[:, :, None] * picked, axis=1)
    expert_out = summed.astype(jnp.bfloat16).reshape(per_dev, 2, width)
    return (cache_out, attn_out, expert_out)


def flip(value, mask):
    out, bit = value, 1
    while bit <= mask:
        if mask & bit:
            out = out + bit - 2 * bit * ((value // bit) % 2)
        bit *= 2
    return out


def fused_kernel(
    ep_count,
    per_dev,
    heads,
    tok_in,
    gain_ref,
    routes_ref,
    gates_ref,
    anc_ref,
    new_ref,
    cache_ref,
    q_hbm,
    prompt_hbm,
    win_hbm,
    wout_hbm,
    cache_out,
    attn_out,
    exp_out,
    tok_f,
    top_i,
    top_f,
    rows_buf,
    part,
    ra,
    rb1,
    rb2,
    rc,
    anc_buf,
    anc_smem,
    piece_buf,
    chosen,
    win_raw,
    win,
    wout,
    q_ref,
    prompt_raw,
    wide,
    prompt_ref,
    gen_ref,
    own_ref,
    w_sem,
    ag_send,
    ag_recv,
    anc_send,
    anc_recv,
    c1_send,
    c1_recv,
    c2_send,
    c2_recv,
    rs_send,
    rs_recv,
):
    r = lax.axis_index("rep")
    e = lax.axis_index("ep")
    nz = ep_count // 4
    blk = rows_buf.shape[1]
    width = gain_ref.shape[1]
    hid = wout.shape[0]
    hd = q_ref.shape[-1]
    kvh = heads[1]
    kv_rows = 2 * kvh
    c = e % 2
    swap = c if SPLIT else 0
    xstep = 2 - 4 * ((e // 2) % 2)
    ystep = 1 - 2 * r
    f_dev = (r + swap * ystep, e + (1 - swap) * xstep)
    g_dev = (r + (1 - swap) * ystep, e + swap * xstep)
    partner = (r, e + 1 - 2 * c)

    def z_dev(dz):
        return (r, flip(e // 4, dz) * 4 + e % 4)

    def remote(src, dst, ssem, rsem, dev):
        return pltpu.make_async_remote_copy(
            src_ref=src, dst_ref=dst, send_sem=ssem, recv_sem=rsem, device_id=dev, device_id_type=MESH
        )

    win_copies = [
        pltpu.make_async_copy(win_hbm.at[:, :, pl.ds(t * 128, 128)], win_raw.at[t], w_sem.at[4 + PARTS + t])
        for t in range(win_raw.shape[0])
    ]
    wout_copy = pltpu.make_async_copy(wout_hbm, wout, w_sem.at[1])
    q_copy = pltpu.make_async_copy(q_hbm, q_ref, w_sem.at[2])
    prompt_copy = pltpu.make_async_copy(prompt_hbm, prompt_raw, w_sem.at[3])
    piece_copies = [
        pltpu.make_async_copy(cache_ref.at[:, h, e], piece_buf[h].at[e], w_sem.at[4 + h])
        for h in range(PARTS)
    ]

    barrier = pltpu.get_barrier_semaphore()
    for k in range(1, ep_count):
        pl.semaphore_signal(barrier, inc=1, device_id=(r, flip(e, k)), device_id_type=MESH)
    pl.semaphore_signal(barrier, inc=1, device_id=(r + ystep, e), device_id_type=MESH)
    for copy in (*win_copies, prompt_copy, wout_copy, q_copy, *piece_copies):
        copy.start()

    for p in range(per_dev):
        tok_f[2 * p : 2 * p + 2] = tok_in[p].astype(jnp.float32)
        top_i[2 * p : 2 * p + 2] = routes_ref[r, p]
        top_f[2 * p : 2 * p + 2] = gates_ref[r, p]
    values = tok_f[...]
    scale = lax.rsqrt(jnp.mean(values * values, axis=-1, keepdims=True) + 1e-06)
    rows_buf[0, :, :width] = (values * scale * gain_ref[...]).astype(jnp.bfloat16)
    lane = lax.broadcasted_iota(jnp.int32, (blk, rows_buf.shape[2] - width), 1)
    dense = jnp.zeros(lane.shape, jnp.float32)
    for k in range(top_i.shape[1]):
        dense += jnp.where(lane % ep_count == top_i[:, k : k + 1], top_f[:, k : k + 1], 0.0)
    high = dense.astype(jnp.bfloat16).astype(jnp.float32)
    tail = jnp.where(lane < ep_count, high, jnp.where(lane < 2 * ep_count, dense - high, 0.0))
    rows_buf[0, :, width:] = tail.astype(jnp.bfloat16)

    pl.semaphore_wait(barrier, ep_count)

    sent = []

    def gather_send(src_slot, dst_slot, dev):
        copy = remote(
            rows_buf.at[src_slot], rows_buf.at[dst_slot], ag_send.at[len(sent)], ag_recv.at[dst_slot], dev
        )
        copy.start()
        sent.append(copy)

    def gather_wait(slot):
        remote(rows_buf.at[0], rows_buf.at[slot], ag_send.at[0], ag_recv.at[slot], partner).wait_recv()

    def spread_own(k):
        if k:
            gather_wait(8 * k)
        gather_send(8 * k, 8 * k + 1, f_dev)
        gather_send(8 * k, 8 * k + 2, g_dev)
        gather_send(8 * k, 8 * k + 4, partner)

    def spread_f(k):
        gather_wait(8 * k + 1)
        gather_send(8 * k + 1, 8 * k + 3, g_dev)
        gather_send(8 * k + 1, 8 * k + 5, partner)

    def spread_g(k):
        for slot in (2, 3):
            gather_wait(8 * k + slot)
            gather_send(8 * k + slot, 8 * k + slot + 4, partner)

    for dz in range(1, nz):
        gather_send(0, 8 * dz, z_dev(dz))
    spread_own(0)

    anc_copies = []
    for k in range(1, ep_count):
        to = (r, flip(e, k))
        anc_copies.append(remote(anc_ref, anc_buf.at[e], anc_send.at[k], anc_recv.at[k], to))
        anc_copies[-1].start()

    first_copies = [[] for _ in range(PARTS)]
    second_copies = [[] for _ in range(PARTS)]

    def peers(at):
        h, dz = at // nz, nz - 1 - at % nz
        return h, [4 * dz + low for low in (3, 2, 1, 0) if 4 * dz + low]

    def first_exchange(at):
        h, masks = peers(at)
        for k in masks:
            peer = flip(e, k)
            at = h * ep_count + k
            first_copies[h].append(
                remote(cache_ref.at[:, h, peer], piece_buf[h].at[e], c1_send.at[at], c1_recv.at[at], (r, peer))
            )
            first_copies[h][-1].start()

    def choose_pieces(h):
        if h == 0:
            anc_buf[pl.ds(e, 1)] = anc_ref[...][None]
            for copy in anc_copies:
                copy.wait()
            anc_local = pltpu.make_async_copy(anc_buf, anc_smem, w_sem.at[0])
            anc_local.start()
            anc_local.wait()
        for copy in first_copies[h]:
            copy.wait_recv()
        piece_copies[h].wait()
        flat = piece_buf[h].reshape(per_dev * ep_count, *piece_buf[h].shape[2:])

        def choose(to, carry):
            for p in range(per_dev):
                chosen[h, to, p] = flat[anc_smem[to, 0, p]]
            return carry

        lax.fori_loop(0, ep_count, choose, 0)
        cache_out[:, h, pl.ds(e, 1)] = chosen[h, pl.ds(e, 1)].reshape(per_dev, 1, *chosen.shape[3:])

    def second_exchange(at):
        h, masks = peers(at)
        for k in masks:
            peer = flip(e, k)
            at = h * ep_count + k
            second_copies[h].append(
                remote(chosen.at[h, peer], cache_out.at[:, h, e], c2_send.at[at], c2_recv.at[at], (r, peer))
            )
            second_copies[h][-1].start()

    def pick_rows(into, kv):
        count = into.shape[1]
        for at in range(kv):
            into[at] = wide[pl.ds(at, count, stride=kv), :].astype(jnp.bfloat16)

    def place_prompt():
        wide[: new_ref.shape[0]] = new_ref[...].astype(jnp.float32)
        pick_rows(own_ref, kv_rows)
        prompt_copy.wait()
        wide[: prompt_raw.shape[0]] = prompt_raw[...].astype(jnp.float32)
        pick_rows(prompt_ref, kv_rows)

    def place_weights(t):
        win_copies[t].wait()
        wide[: 2 * width] = win_raw.at[t].reshape(2 * width, 128)[...].astype(jnp.float32)
        for g in range(2):
            win[:, g * hid + t * 128 : g * hid + (t + 1) * 128] = wide[pl.ds(g, width, stride=2), :].astype(
                jnp.bfloat16
            )

    stages = {}
    rs_at = [0]

    def reduce_send(name, src, dst, dev):
        copy = remote(src, dst, rs_send.at[rs_at[0]], rs_recv.at[rs_at[0]], dev)
        rs_at[0] += 1
        copy.start()
        stages[name] = copy

    def experts(k):
        for slot in range(4, 8):
            gather_wait(8 * k + slot)
        if not stages:
            wout_copy.wait()
        normed = rows_buf[8 * k : 8 * k + 8, :, :width].reshape(8 * blk, width)
        gate_up = jnp.dot(normed, win[...], preferred_element_type=jnp.float32)
        tail = rows_buf[8 * k : 8 * k + 8, :, width:].astype(jnp.float32).reshape(8 * blk, -1)
        lane = lax.broadcasted_iota(jnp.int32, tail.shape, 1)
        mine = (lane == e) | (lane == e + ep_count)
        gates = jnp.sum(jnp.where(mine, tail, 0.0), axis=-1, keepdims=True)
        value = gate_up[:, :hid]
        act = (value * jax.nn.sigmoid(value) * gate_up[:, hid:] * gates).astype(jnp.bfloat16)
        part[k] = jnp.dot(act, wout[...], preferred_element_type=jnp.float32).astype(jnp.bfloat16)
        reduce_send(("a", k), part.at[k, pl.ds(4 * blk, 4 * blk)], ra.at[k], partner)

    def add_in(k, lo, hi, incoming):
        total = part[k, lo:hi].astype(jnp.float32) + incoming[k, lo:hi].astype(jnp.float32)
        part[k, lo:hi] = total.astype(jnp.bfloat16)

    def reduce_g(k):
        stages["a", k].wait_recv()
        add_in(k, 2 * blk, 4 * blk, ra)
        reduce_send(("b1", k), part.at[k, pl.ds(2 * blk, 2 * blk)], rb1.at[k], g_dev)
        add_in(k, 0, 2 * blk, ra)

    def reduce_f(k):
        stages["b1", k].wait_recv()
        add_in(k, blk, 2 * blk, rb1)
        reduce_send(("b2", k), part.at[k, pl.ds(blk, blk)], rb2.at[k], f_dev)
        add_in(k, 0, blk, rb1)

    def reduce_z(k):
        stages["b2", k].wait_recv()
        add_in(k, 0, blk, rb2)
        if k:
            reduce_send(("z", k), part.at[k, pl.ds(0, blk)], rc.at[k], z_dev(k))

    def reduce_end():
        total = part[0, :blk].astype(jnp.float32)
        for k in range(1, nz):
            stages["z", k].wait_recv()
            total = total + rc[k].astype(jnp.float32)
        exp_out[...] = total

    per_kv = heads[0] // kvh
    q_rows = per_dev * 2 * per_kv
    q_at = lax.broadcasted_iota(jnp.int32, (q_rows, 1), 0)
    q_part = q_at // (2 * per_kv)
    q_pos = (q_at // per_kv) % 2
    new_at = lax.broadcasted_iota(jnp.int32, (1, per_dev * 2), 1)
    new_ok = (new_at // 2 == q_part) & (new_at % 2 <= q_pos)
    gen_len = gen_ref.shape[1] // per_dev
    gen_at = lax.broadcasted_iota(jnp.int32, (1, gen_len * per_dev), 1)
    gen_ok = gen_at // gen_len == q_part
    contract = (((1,), (1,)), ((), ()))

    def attention(n):
        q = q_ref[:, :, n * per_kv : (n + 1) * per_kv, :].reshape(q_rows, hd)
        pairs = [
            (prompt_ref[n], prompt_ref[kvh + n], None),
            (gen_ref[n], gen_ref[kvh + n], gen_ok),
            (own_ref[n], own_ref[kvh + n], new_ok),
        ]
        scores = []
        for key, _, ok in pairs:
            score = lax.dot_general(q, key, contract, preferred_element_type=jnp.float32) * (
                1.0 / math.sqrt(hd)
            )
            scores.append(score if ok is None else jnp.where(ok, score, -jnp.inf))
        top = functools.reduce(jnp.maximum, [s.max(-1, keepdims=True) for s in scores])
        exps = [jnp.exp(s - top) for s in scores]
        inv = 1.0 / functools.reduce(jnp.add, [x.sum(-1, keepdims=True) for x in exps])
        total = 0.0
        for x, (_, value, _) in zip(exps, pairs):
            total = total + jnp.dot(
                (x * inv).astype(jnp.bfloat16), value, preferred_element_type=jnp.float32
            )
        attn_out[:, :, n * per_kv : (n + 1) * per_kv, :] = total.astype(jnp.bfloat16).reshape(
            per_dev, 2, per_kv, hd
        )

    def attend_all():
        for h in range(PARTS):
            for copy in second_copies[h]:
                copy.wait_recv()
        q_copy.wait()
        wide[: gen_ref.shape[1] * kv_rows] = (
            cache_out[...].reshape(gen_ref.shape[1] * kv_rows, hd).astype(jnp.float32)
        )
        pick_rows(gen_ref, kv_rows)
        for n in range(kvh):
            attention(n)

    steps = {
        "O": spread_own,
        "F": spread_f,
        "G": spread_g,
        "X": experts,
        "g": reduce_g,
        "f": reduce_f,
        "z": reduce_z,
        "1": first_exchange,
        "H": choose_pieces,
        "2": second_exchange,
        "P": lambda _: place_prompt(),
        "W": place_weights,
        "A": lambda _: attend_all(),
        "E": lambda _: reduce_end(),
    }
    for name in ORDER:
        steps[name[0]](int(name[1:]))

    for copy in sent:
        copy.wait_send()

    for h in range(PARTS):
        for copy in first_copies[h] + second_copies[h]:
            copy.wait_send()
    for copy in stages.values():
        copy.wait_send()


def place_kernel(cache_ref, attn_ref, experts_ref, cache_out, attn_out, experts_out, sem):
    copies = [
        pltpu.make_async_copy(cache_ref, cache_out, sem.at[0]),
        pltpu.make_async_copy(attn_ref, attn_out, sem.at[1]),
    ]
    for copy in copies:
        copy.start()
    for p in range(experts_out.shape[0]):
        experts_out[p] = experts_ref[2 * p : 2 * p + 2].astype(jnp.bfloat16)
    for copy in copies:
        copy.wait()


def dense_shards(
    gen_cache,
    prompt_cache,
    ancestors,
    queries,
    new_kv,
    tokens_in,
    norm_gain,
    routes,
    gate_weights,
    w_gate_up,
    w_down,
):
    ep_count = lax.axis_size("ep")
    per_dev = gen_cache.shape[0]
    width = tokens_in.shape[2]
    hid = w_down.shape[1]
    heads = (queries.shape[2], new_kv.shape[3])
    hd = queries.shape[3]
    nz = ep_count // 4
    blk = 2 * per_dev
    chunk = 8 * blk
    bf = jnp.bfloat16

    kv_rows = 2 * heads[1]
    top_count = routes.shape[3]
    prompt_len = prompt_cache.shape[0]
    gen_rows = per_dev * gen_cache.shape[1]
    piece_rows = gen_cache.size // (per_dev * PARTS * ep_count * hd)
    tiles = hid // 128
    row = width + -(-2 * ep_count // 128) * 128

    def sems(n):
        return pltpu.SemaphoreType.DMA((n,))

    vmem = pl.BlockSpec(memory_space=pltpu.VMEM)
    hbm = pl.BlockSpec(memory_space=pl.ANY)
    cache_new, attn, experts = pl.pallas_call(
        functools.partial(fused_kernel, ep_count, per_dev, heads),
        out_shape=(
            pltpu.VMEM((per_dev, PARTS, ep_count, piece_rows, hd), bf),
            pltpu.VMEM(queries.shape, bf),
            pltpu.VMEM((blk, width), jnp.float32),
        ),
        in_specs=[vmem] * 6 + [pl.BlockSpec(memory_space=pltpu.HBM)] * 5,
        out_specs=(vmem,) * 3,
        scratch_shapes=[
            pltpu.VMEM((blk, width), jnp.float32),
            pltpu.VMEM((blk, top_count), jnp.int32),
            pltpu.VMEM((blk, top_count), jnp.float32),
            pltpu.VMEM((8 * nz, blk, row), bf),
            pltpu.VMEM((nz, chunk, width), bf),
            pltpu.VMEM((nz, chunk // 2, width), bf),
            pltpu.VMEM((nz, chunk // 4, width), bf),
            pltpu.VMEM((nz, chunk // 8, width), bf),
            pltpu.VMEM((nz, blk, width), bf),
            pltpu.VMEM((ep_count, 1, per_dev), jnp.int32),
            pltpu.SMEM((ep_count, 1, per_dev), jnp.int32),
            (pltpu.VMEM((ep_count, per_dev, piece_rows, hd), bf),) * PARTS,
            pltpu.VMEM((PARTS, ep_count, per_dev, piece_rows, hd), bf),
            pltpu.VMEM((tiles, width, 2, 128), bf),
            pltpu.VMEM((width, 2 * hid), bf),
            pltpu.VMEM((hid, width), bf),
            pltpu.VMEM(queries.shape, bf),
            pltpu.VMEM((prompt_len * kv_rows, hd), bf),
            pltpu.VMEM((max(prompt_len * kv_rows, gen_rows * kv_rows, 2 * width), hd), jnp.float32),
            pltpu.VMEM((kv_rows, prompt_len, hd), bf),
            pltpu.VMEM((kv_rows, gen_rows, hd), bf),
            pltpu.VMEM((kv_rows, blk, hd), bf),
            sems(4 + PARTS + tiles),
            sems(8 * nz),
            sems(8 * nz),
            sems(ep_count),
            sems(ep_count),
            sems(PARTS * ep_count),
            sems(PARTS * ep_count),
            sems(PARTS * ep_count),
            sems(PARTS * ep_count),
            sems(4 * nz),
            sems(4 * nz),
        ],
        compiler_params=pltpu.CompilerParams(collective_id=0, has_side_effects=True, vmem_limit_bytes=40 * 2**20),
        name="resample_attend_experts",
    )(
        *(
            pltpu.with_memory_space_constraint(x, pltpu.HBM)
            for x in (
                tokens_in,
                norm_gain.reshape(1, width),
                routes,
                gate_weights,
                ancestors.reshape(1, per_dev),
                new_kv.reshape(blk * kv_rows, hd),
                gen_cache.reshape(per_dev, PARTS, ep_count, piece_rows, hd),
                queries,
                prompt_cache.reshape(prompt_len * kv_rows, hd),
                w_gate_up.reshape(width, 2, hid),
                w_down.reshape(hid, width),
            )
        ),
    )
    cache_last, attn_last, experts_last = pl.pallas_call(
        place_kernel,
        out_shape=(
            jax.ShapeDtypeStruct(cache_new.shape, bf),
            jax.ShapeDtypeStruct(attn.shape, bf),
            jax.ShapeDtypeStruct(tokens_in.shape, bf),
        ),
        in_specs=[vmem] * 3,
        out_specs=(hbm, hbm, vmem),
        scratch_shapes=[sems(2)],
        name="place_outputs",
    )(*(pltpu.with_memory_space_constraint(x, pltpu.VMEM) for x in (cache_new, attn, experts)))
    return (cache_last.reshape(gen_cache.shape), attn_last, experts_last)


def fits_dense(rep_count, ep_count, per_dev, width, hid):
    if rep_count != 2 or ep_count != 16 or hid % 128:
        return False
    row_bytes = rep_count * ep_count * 2 * per_dev * width * 2
    return 6 * row_bytes + 6 * width * hid < 40 * 2**20


def shards(*args):
    gen_cache, tokens_in, w_down = args[0], args[5], args[10]
    dense = fits_dense(
        lax.axis_size("rep"), lax.axis_size("ep"), gen_cache.shape[0], tokens_in.shape[2], w_down.shape[1]
    )
    return dense_shards(*args) if dense else routed_shards(*args)


def solution(mesh):
    placed = (
        P(("rep", "ep"), None, None, None, None),
        P(),
        P(("rep", "ep")),
        P(("rep", "ep"), None, None, None),
        P(("rep", "ep"), None, None, None, None),
        P(("rep", "ep"), None, None),
        P(),
        P(None, "ep", None, None),
        P(None, "ep", None, None),
        P("ep", None, None, "rep"),
        P("ep", "rep", None),
    )
    return jax.shard_map(
        shards,
        mesh=mesh,
        in_specs=placed,
        out_specs=(
            P(("rep", "ep"), None, None, None, None),
            P(("rep", "ep"), None, None, None),
            P(("rep", "ep"), None, None),
        ),
        check_vma=False,
    )
```

```python
import functools
import math

import jax
import jax.numpy as jnp
from jax import lax
from jax.experimental import pallas as pl
from jax.experimental.pallas import tpu as pltpu
from jax.sharding import PartitionSpec as P

MESH = pl.DeviceIdType.MESH
PARTS = 2
SPLIT = False
ORDER = (
    "F0", "14", "W2", "O1", "W1", "11", "O2", "F1",
    "W0", "O3", "F2", "10", "12", "G1", "13", "G0",
    "X1", "17", "15", "16", "F3", "g1", "H0", "G2",
    "21", "22", "20", "X2", "H1", "27", "g2", "25",
    "G3", "f1", "X3", "X0", "g3", "26", "g0", "23",
    "f2", "24", "z2", "f3", "P0", "z3", "f0", "z1",
    "A0", "z0", "E0",
)


def attend(queries, gen_block, new_block, prompt_cache):
    count = queries.shape[0]
    heads = queries.shape[2]
    head_dim = queries.shape[3]
    kv_heads = new_block.shape[3]
    score_scale = 1.0 / math.sqrt(head_dim)
    grouped = queries.reshape(count, 2, kv_heads, heads // kv_heads, head_dim)
    prompt_scores = (
        jnp.einsum(
            "btngd,snd->btngs", grouped, prompt_cache[:, 0], preferred_element_type=jnp.float32
        )
        * score_scale
    )
    gen_scores = (
        jnp.einsum(
            "btngd,bsnd->btngs", grouped, gen_block[:, :, 0], preferred_element_type=jnp.float32
        )
        * score_scale
    )
    new_scores = (
        jnp.einsum(
            "btngd,bsnd->btngs", grouped, new_block[:, :, 0], preferred_element_type=jnp.float32
        )
        * score_scale
    )
    causal = lax.broadcasted_iota(jnp.int32, (2, 2), 1) <= lax.broadcasted_iota(
        jnp.int32, (2, 2), 0
    )
    new_scores = jnp.where(causal[None, :, None, None, :], new_scores, -jnp.inf)
    row_max = jnp.maximum(
        jnp.maximum(prompt_scores.max(-1), gen_scores.max(-1)), new_scores.max(-1)
    )[..., None]
    prompt_exp = jnp.exp(prompt_scores - row_max)
    gen_exp = jnp.exp(gen_scores - row_max)
    new_exp = jnp.exp(new_scores - row_max)
    denom = (prompt_exp.sum(-1) + gen_exp.sum(-1) + new_exp.sum(-1))[..., None]
    prompt_weights = (prompt_exp / denom).astype(jnp.bfloat16)
    gen_weights = (gen_exp / denom).astype(jnp.bfloat16)
    new_weights = (new_exp / denom).astype(jnp.bfloat16)
    result = jnp.einsum(
        "btngs,snd->btngd", prompt_weights, prompt_cache[:, 1], preferred_element_type=jnp.float32
    )
    result = result + jnp.einsum(
        "btngs,bsnd->btngd", gen_weights, gen_block[:, :, 1], preferred_element_type=jnp.float32
    )
    result = result + jnp.einsum(
        "btngs,bsnd->btngd", new_weights, new_block[:, :, 1], preferred_element_type=jnp.float32
    )
    return result.reshape(count, 2, heads, head_dim).astype(jnp.bfloat16)


def slot_numbers(expert_ids, capacity):
    flat_ids = expert_ids.reshape(-1)
    place = jnp.arange(flat_ids.shape[0], dtype=jnp.int32)
    earlier = place[None, :] < place[:, None]
    same = flat_ids[None, :] == flat_ids[:, None]
    rank = jnp.sum((same & earlier).astype(jnp.int32), axis=1)
    return (flat_ids * capacity + rank).reshape(expert_ids.shape)


def pack_rows(rows, slot_ids, slot_count):
    selector = (
        (jnp.arange(slot_count, dtype=jnp.int32)[:, None, None] == slot_ids[None, :, :])
        .any(-1)
        .astype(jnp.bfloat16)
    )
    return jnp.dot(selector, rows, preferred_element_type=jnp.float32).astype(jnp.bfloat16)


def routed_shards(
    gen_cache,
    prompt_cache,
    ancestors,
    queries,
    new_kv,
    tokens_in,
    norm_gain,
    routes,
    gate_weights,
    w_gate_up,
    w_down,
):
    ep_count = lax.axis_size("ep")
    rep_count = lax.axis_size("rep")
    per_dev = gen_cache.shape[0]
    width = tokens_in.shape[2]
    top_count = routes.shape[3]
    parents = lax.all_gather(ancestors, "ep", axis=0, tiled=True)
    piece_len = gen_cache.size // (per_dev * ep_count)
    flat_cache = gen_cache.reshape(per_dev, ep_count, piece_len)
    chosen = jnp.take(
        lax.all_to_all(flat_cache, "ep", split_axis=1, concat_axis=0, tiled=True), parents, axis=0
    )
    moved = lax.all_to_all(chosen, "ep", split_axis=0, concat_axis=1, tiled=True)
    cache_out = moved.reshape(gen_cache.shape)
    attn_out = attend(queries, cache_out, new_kv, prompt_cache)
    values_f = tokens_in.astype(jnp.float32).reshape(per_dev * 2, width)
    normed = (
        values_f
        * lax.rsqrt(jnp.mean(values_f * values_f, axis=-1, keepdims=True) + 1e-06)
        * norm_gain
    ).astype(jnp.bfloat16)
    half_cols = w_down.shape[1]
    weight_in = w_gate_up.reshape(width, 2 * half_cols)
    weight_out = w_down.reshape(half_cols, width)
    per_expert = min(2 * per_dev, 2 * ((2 * per_dev * top_count + ep_count - 1) // ep_count))
    rep_place = lax.axis_index("rep")
    own_routes = lax.dynamic_index_in_dim(routes, rep_place, 0, keepdims=False).reshape(
        -1, top_count
    )
    own_gates = lax.dynamic_index_in_dim(gate_weights, rep_place, 0, keepdims=False).reshape(
        -1, top_count
    )
    slot_ids = slot_numbers(own_routes, per_expert)
    outgoing = pack_rows(normed, slot_ids, ep_count * per_expert).reshape(
        ep_count, per_expert, width
    )
    received = lax.all_to_all(outgoing, "ep", split_axis=0, concat_axis=0, tiled=True)
    all_rows = lax.all_gather(received, "rep", axis=0, tiled=True)
    gate_up = jnp.dot(all_rows.reshape(-1, width), weight_in, preferred_element_type=jnp.float32)
    act = (jax.nn.silu(gate_up[:, :half_cols]) * gate_up[:, half_cols:]).astype(jnp.bfloat16)
    produced = (
        jnp.dot(act, weight_out, preferred_element_type=jnp.float32)
        .astype(jnp.bfloat16)
        .reshape(all_rows.shape)
    )
    parts_back = lax.all_to_all(produced, "rep", split_axis=0, concat_axis=0, tiled=True)
    added = jnp.sum(parts_back.astype(jnp.float32).reshape((rep_count,) + received.shape), axis=0)
    came_back = (
        lax.all_to_all(added.astype(jnp.bfloat16), "ep", split_axis=0, concat_axis=0, tiled=True)
        .astype(added.dtype)
        .reshape(-1, width)
    )
    picked = jnp.take(came_back, slot_ids, axis=0)
    summed = jnp.sum(own_gates[:, :, None] * picked, axis=1)
    expert_out = summed.astype(jnp.bfloat16).reshape(per_dev, 2, width)
    return (cache_out, attn_out, expert_out)


def flip(value, mask):
    out, bit = value, 1
    while bit <= mask:
        if mask & bit:
            out = out + bit - 2 * bit * ((value // bit) % 2)
        bit *= 2
    return out


def fused_kernel(
    ep_count,
    per_dev,
    heads,
    tok_in,
    gain_ref,
    routes_ref,
    gates_ref,
    anc_ref,
    new_ref,
    cache_ref,
    q_hbm,
    prompt_hbm,
    win_hbm,
    wout_hbm,
    cache_out,
    attn_out,
    exp_out,
    tok_f,
    top_i,
    top_f,
    rows_buf,
    part,
    ra,
    rb1,
    rb2,
    rc,
    anc_buf,
    anc_smem,
    piece_buf,
    chosen,
    win_raw,
    win,
    wout,
    q_ref,
    prompt_raw,
    wide,
    prompt_ref,
    gen_ref,
    own_ref,
    w_sem,
    ag_send,
    ag_recv,
    anc_send,
    anc_recv,
    c1_send,
    c1_recv,
    c2_send,
    c2_recv,
    rs_send,
    rs_recv,
):
    r = lax.axis_index("rep")
    e = lax.axis_index("ep")
    nz = ep_count // 4
    blk = rows_buf.shape[1]
    width = gain_ref.shape[1]
    hid = wout.shape[0]
    hd = q_ref.shape[-1]
    kvh = heads[1]
    kv_rows = 2 * kvh
    c = e % 2
    swap = c if SPLIT else 0
    xstep = 2 - 4 * ((e // 2) % 2)
    ystep = 1 - 2 * r
    f_dev = (r + swap * ystep, e + (1 - swap) * xstep)
    g_dev = (r + (1 - swap) * ystep, e + swap * xstep)
    partner = (r, e + 1 - 2 * c)

    def z_dev(dz):
        return (r, flip(e // 4, dz) * 4 + e % 4)

    def remote(src, dst, ssem, rsem, dev):
        return pltpu.make_async_remote_copy(
            src_ref=src, dst_ref=dst, send_sem=ssem, recv_sem=rsem, device_id=dev, device_id_type=MESH
        )

    win_copies = [
        pltpu.make_async_copy(win_hbm.at[:, :, pl.ds(t * 128, 128)], win_raw.at[t], w_sem.at[4 + PARTS + t])
        for t in range(win_raw.shape[0])
    ]
    wout_copy = pltpu.make_async_copy(wout_hbm, wout, w_sem.at[1])
    q_copy = pltpu.make_async_copy(q_hbm, q_ref, w_sem.at[2])
    prompt_copy = pltpu.make_async_copy(prompt_hbm, prompt_raw, w_sem.at[3])
    piece_copies = [
        pltpu.make_async_copy(cache_ref.at[:, h, e], piece_buf[h].at[e], w_sem.at[4 + h])
        for h in range(PARTS)
    ]

    barrier = pltpu.get_barrier_semaphore()
    for k in range(1, ep_count):
        pl.semaphore_signal(barrier, inc=1, device_id=(r, flip(e, k)), device_id_type=MESH)
    pl.semaphore_signal(barrier, inc=1, device_id=(r + ystep, e), device_id_type=MESH)
    for copy in (*win_copies, prompt_copy, wout_copy, q_copy, *piece_copies):
        copy.start()

    for p in range(per_dev):
        tok_f[2 * p : 2 * p + 2] = tok_in[p].astype(jnp.float32)
        top_i[2 * p : 2 * p + 2] = routes_ref[r, p]
        top_f[2 * p : 2 * p + 2] = gates_ref[r, p]
    values = tok_f[...]
    scale = lax.rsqrt(jnp.mean(values * values, axis=-1, keepdims=True) + 1e-06)
    rows_buf[0, :, :width] = (values * scale * gain_ref[...]).astype(jnp.bfloat16)
    lane = lax.broadcasted_iota(jnp.int32, (blk, rows_buf.shape[2] - width), 1)
    dense = jnp.zeros(lane.shape, jnp.float32)
    for k in range(top_i.shape[1]):
        dense += jnp.where(lane % ep_count == top_i[:, k : k + 1], top_f[:, k : k + 1], 0.0)
    high = dense.astype(jnp.bfloat16).astype(jnp.float32)
    tail = jnp.where(lane < ep_count, high, jnp.where(lane < 2 * ep_count, dense - high, 0.0))
    rows_buf[0, :, width:] = tail.astype(jnp.bfloat16)

    pl.semaphore_wait(barrier, ep_count)

    sent = []

    def gather_send(src_slot, dst_slot, dev):
        copy = remote(
            rows_buf.at[src_slot], rows_buf.at[dst_slot], ag_send.at[len(sent)], ag_recv.at[dst_slot], dev
        )
        copy.start()
        sent.append(copy)

    def gather_wait(slot):
        remote(rows_buf.at[0], rows_buf.at[slot], ag_send.at[0], ag_recv.at[slot], partner).wait_recv()

    def spread_own(k):
        if k:
            gather_wait(8 * k)
        gather_send(8 * k, 8 * k + 1, f_dev)
        gather_send(8 * k, 8 * k + 2, g_dev)
        gather_send(8 * k, 8 * k + 4, partner)

    def spread_f(k):
        gather_wait(8 * k + 1)
        gather_send(8 * k + 1, 8 * k + 3, g_dev)
        gather_send(8 * k + 1, 8 * k + 5, partner)

    def spread_g(k):
        for slot in (2, 3):
            gather_wait(8 * k + slot)
            gather_send(8 * k + slot, 8 * k + slot + 4, partner)

    for dz in range(1, nz):
        gather_send(0, 8 * dz, z_dev(dz))
    spread_own(0)

    anc_copies = []
    for k in range(1, ep_count):
        to = (r, flip(e, k))
        anc_copies.append(remote(anc_ref, anc_buf.at[e], anc_send.at[k], anc_recv.at[k], to))
        anc_copies[-1].start()

    first_copies = [[] for _ in range(PARTS)]
    second_copies = [[] for _ in range(PARTS)]

    def peers(at):
        h, dz = at // nz, nz - 1 - at % nz
        return h, [4 * dz + low for low in (3, 2, 1, 0) if 4 * dz + low]

    def first_exchange(at):
        h, masks = peers(at)
        for k in masks:
            peer = flip(e, k)
            at = h * ep_count + k
            first_copies[h].append(
                remote(cache_ref.at[:, h, peer], piece_buf[h].at[e], c1_send.at[at], c1_recv.at[at], (r, peer))
            )
            first_copies[h][-1].start()

    def choose_pieces(h):
        if h == 0:
            anc_buf[pl.ds(e, 1)] = anc_ref[...][None]
            for copy in anc_copies:
                copy.wait()
            anc_local = pltpu.make_async_copy(anc_buf, anc_smem, w_sem.at[0])
            anc_local.start()
            anc_local.wait()
        for copy in first_copies[h]:
            copy.wait_recv()
        piece_copies[h].wait()
        flat = piece_buf[h].reshape(per_dev * ep_count, *piece_buf[h].shape[2:])

        def choose(to, carry):
            for p in range(per_dev):
                chosen[h, to, p] = flat[anc_smem[to, 0, p]]
            return carry

        lax.fori_loop(0, ep_count, choose, 0)
        cache_out[:, h, pl.ds(e, 1)] = chosen[h, pl.ds(e, 1)].reshape(per_dev, 1, *chosen.shape[3:])

    def second_exchange(at):
        h, masks = peers(at)
        for k in masks:
            peer = flip(e, k)
            at = h * ep_count + k
            second_copies[h].append(
                remote(chosen.at[h, peer], cache_out.at[:, h, e], c2_send.at[at], c2_recv.at[at], (r, peer))
            )
            second_copies[h][-1].start()

    def pick_rows(into, kv):
        count = into.shape[1]
        for at in range(kv):
            into[at] = wide[pl.ds(at, count, stride=kv), :].astype(jnp.bfloat16)

    def place_prompt():
        wide[: new_ref.shape[0]] = new_ref[...].astype(jnp.float32)
        pick_rows(own_ref, kv_rows)
        prompt_copy.wait()
        wide[: prompt_raw.shape[0]] = prompt_raw[...].astype(jnp.float32)
        pick_rows(prompt_ref, kv_rows)

    def place_weights(t):
        win_copies[t].wait()
        wide[: 2 * width] = win_raw.at[t].reshape(2 * width, 128)[...].astype(jnp.float32)
        for g in range(2):
            win[:, g * hid + t * 128 : g * hid + (t + 1) * 128] = wide[pl.ds(g, width, stride=2), :].astype(
                jnp.bfloat16
            )

    stages = {}
    rs_at = [0]

    def reduce_send(name, src, dst, dev):
        copy = remote(src, dst, rs_send.at[rs_at[0]], rs_recv.at[rs_at[0]], dev)
        rs_at[0] += 1
        copy.start()
        stages[name] = copy

    def experts(k):
        for slot in range(4, 8):
            gather_wait(8 * k + slot)
        if not stages:
            wout_copy.wait()
        normed = rows_buf[8 * k : 8 * k + 8, :, :width].reshape(8 * blk, width)
        gate_up = jnp.dot(normed, win[...], preferred_element_type=jnp.float32)
        tail = rows_buf[8 * k : 8 * k + 8, :, width:].astype(jnp.float32).reshape(8 * blk, -1)
        lane = lax.broadcasted_iota(jnp.int32, tail.shape, 1)
        mine = (lane == e) | (lane == e + ep_count)
        gates = jnp.sum(jnp.where(mine, tail, 0.0), axis=-1, keepdims=True)
        value = gate_up[:, :hid]
        act = (value * jax.nn.sigmoid(value) * gate_up[:, hid:] * gates).astype(jnp.bfloat16)
        part[k] = jnp.dot(act, wout[...], preferred_element_type=jnp.float32).astype(jnp.bfloat16)
        reduce_send(("a", k), part.at[k, pl.ds(4 * blk, 4 * blk)], ra.at[k], partner)

    def add_in(k, lo, hi, incoming):
        total = part[k, lo:hi].astype(jnp.float32) + incoming[k, lo:hi].astype(jnp.float32)
        part[k, lo:hi] = total.astype(jnp.bfloat16)

    def reduce_g(k):
        stages["a", k].wait_recv()
        add_in(k, 2 * blk, 4 * blk, ra)
        reduce_send(("b1", k), part.at[k, pl.ds(2 * blk, 2 * blk)], rb1.at[k], g_dev)
        add_in(k, 0, 2 * blk, ra)

    def reduce_f(k):
        stages["b1", k].wait_recv()
        add_in(k, blk, 2 * blk, rb1)
        reduce_send(("b2", k), part.at[k, pl.ds(blk, blk)], rb2.at[k], f_dev)
        add_in(k, 0, blk, rb1)

    def reduce_z(k):
        stages["b2", k].wait_recv()
        add_in(k, 0, blk, rb2)
        if k:
            reduce_send(("z", k), part.at[k, pl.ds(0, blk)], rc.at[k], z_dev(k))

    def reduce_end():
        total = part[0, :blk].astype(jnp.float32)
        for k in range(1, nz):
            stages["z", k].wait_recv()
            total = total + rc[k].astype(jnp.float32)
        exp_out[...] = total

    per_kv = heads[0] // kvh
    q_rows = per_dev * 2 * per_kv
    q_at = lax.broadcasted_iota(jnp.int32, (q_rows, 1), 0)
    q_part = q_at // (2 * per_kv)
    q_pos = (q_at // per_kv) % 2
    new_at = lax.broadcasted_iota(jnp.int32, (1, per_dev * 2), 1)
    new_ok = (new_at // 2 == q_part) & (new_at % 2 <= q_pos)
    gen_len = gen_ref.shape[1] // per_dev
    gen_at = lax.broadcasted_iota(jnp.int32, (1, gen_len * per_dev), 1)
    gen_ok = gen_at // gen_len == q_part
    contract = (((1,), (1,)), ((), ()))

    def attention(n):
        q = q_ref[:, :, n * per_kv : (n + 1) * per_kv, :].reshape(q_rows, hd)
        pairs = [
            (prompt_ref[n], prompt_ref[kvh + n], None),
            (gen_ref[n], gen_ref[kvh + n], gen_ok),
            (own_ref[n], own_ref[kvh + n], new_ok),
        ]
        scores = []
        for key, _, ok in pairs:
            score = lax.dot_general(q, key, contract, preferred_element_type=jnp.float32) * (
                1.0 / math.sqrt(hd)
            )
            scores.append(score if ok is None else jnp.where(ok, score, -jnp.inf))
        top = functools.reduce(jnp.maximum, [s.max(-1, keepdims=True) for s in scores])
        exps = [jnp.exp(s - top) for s in scores]
        inv = 1.0 / functools.reduce(jnp.add, [x.sum(-1, keepdims=True) for x in exps])
        total = 0.0
        for x, (_, value, _) in zip(exps, pairs):
            total = total + jnp.dot(
                (x * inv).astype(jnp.bfloat16), value, preferred_element_type=jnp.float32
            )
        attn_out[:, :, n * per_kv : (n + 1) * per_kv, :] = total.astype(jnp.bfloat16).reshape(
            per_dev, 2, per_kv, hd
        )

    def attend_all():
        for h in range(PARTS):
            for copy in second_copies[h]:
                copy.wait_recv()
        q_copy.wait()
        wide[: gen_ref.shape[1] * kv_rows] = (
            cache_out[...].reshape(gen_ref.shape[1] * kv_rows, hd).astype(jnp.float32)
        )
        pick_rows(gen_ref, kv_rows)
        for n in range(kvh):
            attention(n)

    steps = {
        "O": spread_own,
        "F": spread_f,
        "G": spread_g,
        "X": experts,
        "g": reduce_g,
        "f": reduce_f,
        "z": reduce_z,
        "1": first_exchange,
        "H": choose_pieces,
        "2": second_exchange,
        "P": lambda _: place_prompt(),
        "W": place_weights,
        "A": lambda _: attend_all(),
        "E": lambda _: reduce_end(),
    }
    for name in ORDER:
        steps[name[0]](int(name[1:]))

    for copy in sent:
        copy.wait_send()

    for h in range(PARTS):
        for copy in first_copies[h] + second_copies[h]:
            copy.wait_send()
    for copy in stages.values():
        copy.wait_send()


def place_kernel(cache_ref, attn_ref, experts_ref, cache_out, attn_out, experts_out, sem):
    copies = [
        pltpu.make_async_copy(cache_ref, cache_out, sem.at[0]),
        pltpu.make_async_copy(attn_ref, attn_out, sem.at[1]),
    ]
    for copy in copies:
        copy.start()
    for p in range(experts_out.shape[0]):
        experts_out[p] = experts_ref[2 * p : 2 * p + 2].astype(jnp.bfloat16)
    for copy in copies:
        copy.wait()


def dense_shards(
    gen_cache,
    prompt_cache,
    ancestors,
    queries,
    new_kv,
    tokens_in,
    norm_gain,
    routes,
    gate_weights,
    w_gate_up,
    w_down,
):
    ep_count = lax.axis_size("ep")
    per_dev = gen_cache.shape[0]
    width = tokens_in.shape[2]
    hid = w_down.shape[1]
    heads = (queries.shape[2], new_kv.shape[3])
    hd = queries.shape[3]
    nz = ep_count // 4
    blk = 2 * per_dev
    chunk = 8 * blk
    bf = jnp.bfloat16

    kv_rows = 2 * heads[1]
    top_count = routes.shape[3]
    prompt_len = prompt_cache.shape[0]
    gen_rows = per_dev * gen_cache.shape[1]
    piece_rows = gen_cache.size // (per_dev * PARTS * ep_count * hd)
    tiles = hid // 128
    row = width + -(-2 * ep_count // 128) * 128

    def sems(n):
        return pltpu.SemaphoreType.DMA((n,))

    vmem = pl.BlockSpec(memory_space=pltpu.VMEM)
    hbm = pl.BlockSpec(memory_space=pl.ANY)
    cache_new, attn, experts = pl.pallas_call(
        functools.partial(fused_kernel, ep_count, per_dev, heads),
        out_shape=(
            pltpu.VMEM((per_dev, PARTS, ep_count, piece_rows, hd), bf),
            pltpu.VMEM(queries.shape, bf),
            pltpu.VMEM((blk, width), jnp.float32),
        ),
        in_specs=[vmem] * 6 + [pl.BlockSpec(memory_space=pltpu.HBM)] * 5,
        out_specs=(vmem,) * 3,
        scratch_shapes=[
            pltpu.VMEM((blk, width), jnp.float32),
            pltpu.VMEM((blk, top_count), jnp.int32),
            pltpu.VMEM((blk, top_count), jnp.float32),
            pltpu.VMEM((8 * nz, blk, row), bf),
            pltpu.VMEM((nz, chunk, width), bf),
            pltpu.VMEM((nz, chunk // 2, width), bf),
            pltpu.VMEM((nz, chunk // 4, width), bf),
            pltpu.VMEM((nz, chunk // 8, width), bf),
            pltpu.VMEM((nz, blk, width), bf),
            pltpu.VMEM((ep_count, 1, per_dev), jnp.int32),
            pltpu.SMEM((ep_count, 1, per_dev), jnp.int32),
            (pltpu.VMEM((ep_count, per_dev, piece_rows, hd), bf),) * PARTS,
            pltpu.VMEM((PARTS, ep_count, per_dev, piece_rows, hd), bf),
            pltpu.VMEM((tiles, width, 2, 128), bf),
            pltpu.VMEM((width, 2 * hid), bf),
            pltpu.VMEM((hid, width), bf),
            pltpu.VMEM(queries.shape, bf),
            pltpu.VMEM((prompt_len * kv_rows, hd), bf),
            pltpu.VMEM((max(prompt_len * kv_rows, gen_rows * kv_rows, 2 * width), hd), jnp.float32),
            pltpu.VMEM((kv_rows, prompt_len, hd), bf),
            pltpu.VMEM((kv_rows, gen_rows, hd), bf),
            pltpu.VMEM((kv_rows, blk, hd), bf),
            sems(4 + PARTS + tiles),
            sems(8 * nz),
            sems(8 * nz),
            sems(ep_count),
            sems(ep_count),
            sems(PARTS * ep_count),
            sems(PARTS * ep_count),
            sems(PARTS * ep_count),
            sems(PARTS * ep_count),
            sems(4 * nz),
            sems(4 * nz),
        ],
        compiler_params=pltpu.CompilerParams(collective_id=0, has_side_effects=True, vmem_limit_bytes=40 * 2**20),
        name="resample_attend_experts",
    )(
        *(
            pltpu.with_memory_space_constraint(x, pltpu.HBM)
            for x in (
                tokens_in,
                norm_gain.reshape(1, width),
                routes,
                gate_weights,
                ancestors.reshape(1, per_dev),
                new_kv.reshape(blk * kv_rows, hd),
                gen_cache.reshape(per_dev, PARTS, ep_count, piece_rows, hd),
                queries,
                prompt_cache.reshape(prompt_len * kv_rows, hd),
                w_gate_up.reshape(width, 2, hid),
                w_down.reshape(hid, width),
            )
        ),
    )
    cache_last, attn_last, experts_last = pl.pallas_call(
        place_kernel,
        out_shape=(
            jax.ShapeDtypeStruct(cache_new.shape, bf),
            jax.ShapeDtypeStruct(attn.shape, bf),
            jax.ShapeDtypeStruct(tokens_in.shape, bf),
        ),
        in_specs=[vmem] * 3,
        out_specs=(hbm, hbm, vmem),
        scratch_shapes=[sems(2)],
        name="place_outputs",
    )(*(pltpu.with_memory_space_constraint(x, pltpu.VMEM) for x in (cache_new, attn, experts)))
    return (cache_last.reshape(gen_cache.shape), attn_last, experts_last)


def fits_dense(rep_count, ep_count, per_dev, width, hid):
    if rep_count != 2 or ep_count != 16 or hid % 128:
        return False
    row_bytes = rep_count * ep_count * 2 * per_dev * width * 2
    return 6 * row_bytes + 6 * width * hid < 40 * 2**20


def shards(*args):
    gen_cache, tokens_in, w_down = args[0], args[5], args[10]
    dense = fits_dense(
        lax.axis_size("rep"), lax.axis_size("ep"), gen_cache.shape[0], tokens_in.shape[2], w_down.shape[1]
    )
    return dense_shards(*args) if dense else routed_shards(*args)


def solution(mesh):
    placed = (
        P(("rep", "ep"), None, None, None, None),
        P(),
        P(("rep", "ep")),
        P(("rep", "ep"), None, None, None),
        P(("rep", "ep"), None, None, None, None),
        P(("rep", "ep"), None, None),
        P(),
        P(None, "ep", None, None),
        P(None, "ep", None, None),
        P("ep", None, None, "rep"),
        P("ep", "rep", None),
    )
    return jax.shard_map(
        shards,
        mesh=mesh,
        in_specs=placed,
        out_specs=(
            P(("rep", "ep"), None, None, None, None),
            P(("rep", "ep"), None, None, None),
            P(("rep", "ep"), None, None),
        ),
        check_vma=False,
    )
```
